32 devices in a mesh: seq: 8 (over z, y), head: 4 (over x, core).
Axes of the slice: x: 2, y: 2, z: 4, core: 2. Of those that a mesh axis runs over, the one named last changes fastest.
Arguments:
- tokens: bfloat16 [1024, 1024], P('seq'), may hold values from -6 to 6
- cotangent: bfloat16 [1024, 1024], P('seq'), may hold values from -6 to 6
- gate_code: int32 [2, 1024, 8], P(None, 'seq', 'head'), may hold values from 0 to 723000
- beta_code: int32 [2, 1024, 8], P(None, 'seq', 'head'), may hold values from 256 to 1024
- norm1_gain: float32 [2, 1024], replicated, may hold values from 0.5 to 1.5
- weight_in: bfloat16 [2, 1024, 6144], P(None, None, 'head'), may hold values from -0.1875 to 0.1875
- conv_weight: bfloat16 [2, 4, 4096], P(None, None, 'head'), may hold values from -3 to 3
- out_gain: float32 [2, 256], replicated, may hold values from 0.5 to 1.5
- weight_out: bfloat16 [2, 2048, 1024], P(None, 'head'), may hold values from -0.25 to 0.25
- norm2_gain: float32 [2, 1024], replicated, may hold values from 0.5 to 1.5
- weight_gate: bfloat16 [2, 1024, 2816], P(None, None, 'head'), may hold values from -0.1875 to 0.1875
- weight_up: bfloat16 [2, 1024, 2816], P(None, None, 'head'), may hold values from -0.1875 to 0.1875
- weight_down: bfloat16 [2, 2816, 1024], P(None, 'head'), may hold values from -0.21875 to 0.21875
Outputs:
- activations: bfloat16 [1024, 1024], P('seq')
- input_grad: float32 [1024, 1024], P('seq')
- grad_norm1_gain: float32 [2, 1024], replicated
- grad_weight_in: float32 [2, 1024, 6144], P(None, 'seq', 'head')
- grad_conv_weight: float32 [2, 4, 4096], P(None, None, 'head')
- grad_out_gain: float32 [2, 256], replicated
- grad_weight_out: float32 [2, 2048, 1024], P(None, 'head', 'seq')
- grad_norm2_gain: float32 [2, 1024], replicated
- grad_weight_gate: float32 [2, 1024, 2816], P(None, 'seq', 'head')
- grad_weight_up: float32 [2, 1024, 2816], P(None, 'seq', 'head')
- grad_weight_down: float32 [2, 2816, 1024], P(None, 'head', 'seq')
The draws below stay inside these ranges and needn't reach their ends.
All inputs are finite; a program needn't handle non-finite values.
Results may differ from the reference program's by a relative error of at most 0.02.
Values sent between devices are 32-bit elements; how exact they have to be, the bound alone decides.
No kernel may reach another device: no remote copies, remote signals or barrier semaphores. Data moves between devices by JAX's collectives and lax.ppermute only.
A program may use at most 256 MiB of HBM per device.

```python
import jax
import jax.numpy as jnp
from jax import lax

D = 1024
H = 8
DK = 128
DV = 256
FF = 2816
CONV = 4
SPAN = 64
STACK_LEVELS = 2
TOKENS = 1024


def draw_gate_code(key, part):
    keys_all = jax.random.split(key, 5)
    order = jax.random.permutation(keys_all[0], STACK_LEVELS * H).reshape(STACK_LEVELS, 1, H)
    slow = order % 2 == 0
    slow_top = 2 * (2 ** 19 // TOKENS) + 1
    slow_codes = jax.random.randint(keys_all[1], (STACK_LEVELS, TOKENS, H), 0, slow_top)
    fast_codes = jax.random.randint(keys_all[2], (STACK_LEVELS, TOKENS, H), 40000, 80001)
    target_locations = jax.random.randint(keys_all[3], (STACK_LEVELS, 3, 1, H), 0, TOKENS)
    level_number = jax.random.randint(keys_all[4], (STACK_LEVELS, 3, 1, H), 230000, 723001)
    first = lax.broadcasted_iota(jnp.int32, (STACK_LEVELS, 3, 1, H), 1) == 0
    level_number = jnp.where(first, 723000, level_number)
    slot_numbers = lax.broadcasted_iota(jnp.int32, (STACK_LEVELS, 3, TOKENS, H), 2)
    segment_span = jnp.max(jnp.where(slot_numbers == target_locations, level_number, 0), axis=1)
    initial_shift_amount = jnp.where(slow, slow_codes, fast_codes)
    return jnp.where(segment_span > 0, segment_span, initial_shift_amount).astype(jnp.int32)


def place_ends(result, stream_key, least, largest):
    longest = result.shape.index(max(result.shape))
    spots = []
    for shift in (0, 1):
        where = [jax.random.randint(jax.random.fold_in(stream_key, axis), (), 0, length) for axis, length in enumerate(result.shape)]
        where[longest] = (where[longest] + shift) % result.shape[longest]
        spots.append(tuple(where))
    return result.at[spots[0]].set(least).at[spots[1]].set(largest)


def block_scale(own_key, extent, shards, smallest, high):
    loudness, own = 1.0, jax.random.fold_in(own_key, 6)
    for dim, shards_of in shards:
        heights = jnp.exp(jax.random.uniform(jax.random.fold_in(own, dim), (shards_of,), jnp.float32, smallest / len(shards), high / len(shards)))
        loudness = loudness * jnp.repeat(heights, extent[dim] // shards_of).reshape([-1 if axis == dim else 1 for axis in range(len(extent))])
    return loudness


def gaussian(key, shape, scale, most, cuts=(), kind=jnp.bfloat16):
    level = block_scale(key, shape, cuts, -0.22, 0.18) if cuts else 1.0
    values = jax.random.normal(key, shape, jnp.float32) * scale * level
    return jnp.minimum(jnp.maximum(values, -most), most).astype(kind)


def setup_inputs(seed: int = 0) -> dict:
    splits = jax.random.split(jax.random.key(seed), 14)
    tokens = gaussian(splits[0], (TOKENS, D), 1.0, 6.0, ((0, 8),))
    cotangent = gaussian(splits[1], (TOKENS, D), 1.0, 6.0, ((0, 8),))
    gate_code = draw_gate_code(jax.random.fold_in(splits[13], 71), 0)
    beta_code = place_ends(jax.random.randint(splits[3], (STACK_LEVELS, TOKENS, H), 256, 1025), jax.random.fold_in(splits[3], 1), 256, 1024).astype(jnp.int32)
    norm1_gain = jnp.clip(1.0 + 0.1 * jax.random.normal(splits[4], (STACK_LEVELS, D), jnp.float32), 0.5, 1.5)
    weight_in = gaussian(splits[5], (STACK_LEVELS, D, H * (2 * DK + 2 * DV)), D ** -0.5, 0.1875, ((2, 4),))
    conv_weight = gaussian(splits[6], (STACK_LEVELS, CONV, H * (2 * DK + DV)), CONV ** -0.5, 3.0, ((2, 4),))
    out_gain = jnp.clip(1.0 + 0.1 * jax.random.normal(splits[7], (STACK_LEVELS, DV), jnp.float32), 0.5, 1.5)
    weight_out = gaussian(splits[8], (STACK_LEVELS, H * DV, D), (H * DV // 4) ** -0.5, 0.25, ((1, 4),))
    norm2_gain = jnp.clip(1.0 + 0.1 * jax.random.normal(splits[9], (STACK_LEVELS, D), jnp.float32), 0.5, 1.5)
    weight_gate = gaussian(splits[10], (STACK_LEVELS, D, FF), D ** -0.5, 0.1875, ((2, 4),))
    weight_up = gaussian(splits[11], (STACK_LEVELS, D, FF), D ** -0.5, 0.1875, ((2, 4),))
    weight_down = gaussian(splits[12], (STACK_LEVELS, FF, D), (FF // 4) ** -0.5, 0.21875, ((1, 4),))
    return dict(tokens=tokens, cotangent=cotangent, gate_code=gate_code, beta_code=beta_code, norm1_gain=norm1_gain, weight_in=weight_in, conv_weight=conv_weight, out_gain=out_gain, weight_out=weight_out, norm2_gain=norm2_gain, weight_gate=weight_gate, weight_up=weight_up, weight_down=weight_down)


highest = lax.Precision.HIGHEST
norm_eps = 1e-06
gate_unit = 1.0 / 1048576.0
beta_unit = 1.0 / 1024.0

def rms_norm(stream, gain):
    return stream * lax.rsqrt(lax.optimization_barrier(jnp.mean(stream * stream, axis=-1, keepdims=True)) + norm_eps) * gain

def unit_rows(vectors):
    return vectors * lax.rsqrt(lax.optimization_barrier(jnp.sum(vectors * vectors, axis=-1, keepdims=True)) + norm_eps)

def swiglu(gate_pre, up_pre):
    return jax.nn.silu(gate_pre) * up_pre

def post_mix(outputs, gate_z, gain):
    return rms_norm(outputs, gain) * jax.nn.silu(gate_z)

def mixer_inputs(windowed, conv_taps):
    length_total = windowed.shape[0] - (CONV - 1)
    conv_out = conv_taps[0] * windowed[CONV - 1:]
    for tap_index in range(1, CONV):
        conv_out = conv_out + conv_taps[tap_index] * windowed[CONV - 1 - tap_index:CONV - 1 - tap_index + length_total]
    active = jax.nn.silu(conv_out).reshape(length_total, -1, 2 * DK + DV)
    queries = unit_rows(active[:, :, :DK]) * DK ** (-0.5)
    keys_unit = unit_rows(active[:, :, DK:2 * DK])
    return (queries, keys_unit, active[:, :, 2 * DK:])

def span_step(carry_state, pieces):
    queries, keys_unit, values_in, logdecay, beta_rate = pieces
    block_len = queries.shape[0]
    cumulated = jnp.cumsum(logdecay, axis=0)
    cum_heads = jnp.transpose(cumulated)
    row_index = lax.broadcasted_iota(jnp.int32, (1, block_len, block_len), 1)
    col_index = lax.broadcasted_iota(jnp.int32, (1, block_len, block_len), 2)
    inclusive = row_index >= col_index
    log_ratio = jnp.where(inclusive, cum_heads[:, :, None] - cum_heads[:, None, :], 0.0)
    decay_ratio = jnp.where(inclusive, jnp.exp(log_ratio), 0.0)
    beta_heads = jnp.transpose(beta_rate)
    key_key = jnp.einsum('thd,shd->hts', keys_unit, keys_unit, precision=highest)
    strict_lower = jnp.where(row_index > col_index, beta_heads[:, :, None] * decay_ratio * key_key, 0.0)
    system = strict_lower + jnp.eye(block_len, dtype=strict_lower.dtype)[None]
    decay_all = jnp.exp(cumulated)
    right_side = jnp.concatenate([beta_rate[:, :, None] * values_in, (beta_rate * decay_all)[:, :, None] * keys_unit], axis=2)
    right_side = jnp.transpose(right_side, (1, 0, 2))
    solved_system = lax.linalg.triangular_solve(system, right_side, left_side=True, lower=True)
    val_width = values_in.shape[2]
    new_values = solved_system[:, :, :val_width] - jnp.einsum('htd,hvd->htv', solved_system[:, :, val_width:], carry_state, precision=highest)
    query_key = jnp.einsum('thd,shd->hts', queries, keys_unit, precision=highest)
    mixing = decay_ratio * query_key
    outputs = jnp.transpose(decay_all)[:, :, None] * jnp.einsum('thd,hvd->htv', queries, carry_state, precision=highest)
    outputs = outputs + jnp.einsum('hts,hsv->htv', mixing, new_values, precision=highest)
    to_end = jnp.exp(cumulated[-1][None, :] - cumulated)
    new_state = jnp.exp(cumulated[-1])[:, None, None] * carry_state
    new_state = new_state + jnp.einsum('hsv,shd->hvd', new_values, to_end[:, :, None] * keys_unit, precision=highest)
    return (new_state, jnp.transpose(outputs, (1, 0, 2)))

def delta_rule(queries, keys_unit, values_in, logdecay, beta_rate, carry_state):
    length_total = queries.shape[0]
    block_count = length_total // SPAN

    def blocks(tensor):
        return tensor.reshape((block_count, SPAN) + tensor.shape[1:])
    final_state, outputs = lax.scan(span_step, carry_state, (blocks(queries), blocks(keys_unit), blocks(values_in), blocks(logdecay), blocks(beta_rate)))
    return (outputs.reshape((length_total,) + outputs.shape[2:]), final_state)

def layer_forward(stream, logdecay, beta_rate, weights):
    gain_one, weight_in, conv_weight, out_gain, weight_out, gain_two, weight_gate, weight_up, weight_down = weights
    length_total = stream.shape[0]
    normed = rms_norm(stream, gain_one).astype(jnp.bfloat16)
    projected = jnp.dot(normed.astype(jnp.float32), weight_in.astype(jnp.float32), preferred_element_type=jnp.float32).reshape(length_total, H, 2 * DK + 2 * DV)
    conv_input = projected[:, :, :2 * DK + DV].reshape(length_total, -1)
    gate_z = projected[:, :, 2 * DK + DV:]
    windowed = jnp.concatenate([jnp.zeros((CONV - 1, conv_input.shape[1]), jnp.float32), conv_input], axis=0)
    conv_taps = conv_weight.astype(jnp.float32)
    queries, keys_unit, values_in = mixer_inputs(windowed, conv_taps)
    zero_state = jnp.zeros((H, DV, DK), jnp.float32)
    outputs, final_state = delta_rule(queries, keys_unit, values_in, logdecay, beta_rate, zero_state)
    gated_out = post_mix(outputs, gate_z, out_gain).reshape(length_total, -1).astype(jnp.bfloat16)
    stream_mid = stream + jnp.dot(gated_out.astype(jnp.float32), weight_out.astype(jnp.float32), preferred_element_type=jnp.float32)
    second_normed = rms_norm(stream_mid, gain_two).astype(jnp.bfloat16)
    gate_pre = jnp.dot(second_normed.astype(jnp.float32), weight_gate.astype(jnp.float32), preferred_element_type=jnp.float32)
    up_pre = jnp.dot(second_normed.astype(jnp.float32), weight_up.astype(jnp.float32), preferred_element_type=jnp.float32)
    hidden = swiglu(gate_pre, up_pre).astype(jnp.bfloat16)
    stream_next = stream_mid + jnp.dot(hidden.astype(jnp.float32), weight_down.astype(jnp.float32), preferred_element_type=jnp.float32)
    stored = (stream, normed, windowed, conv_taps, gate_z, queries, keys_unit, values_in, outputs, gated_out, stream_mid, second_normed, gate_pre, up_pre, hidden)
    return (stream_next, stored)

def layer_backward(grad_stream, logdecay, beta_rate, weights, stored):
    gain_one, weight_in, conv_weight, out_gain, weight_out, gain_two, weight_gate, weight_up, weight_down = weights
    stream, normed, windowed, conv_taps, gate_z, queries, keys_unit, values_in, outputs, gated_out, stream_mid, second_normed, gate_pre, up_pre, hidden = stored
    length_total = grad_stream.shape[0]
    back_bf = grad_stream.astype(jnp.bfloat16)
    grad_down = jnp.dot(hidden.T.astype(jnp.float32), back_bf.astype(jnp.float32), preferred_element_type=jnp.float32)
    grad_hidden = jnp.dot(back_bf.astype(jnp.float32), weight_down.T.astype(jnp.float32), preferred_element_type=jnp.float32)
    _, act_pull = jax.vjp(swiglu, gate_pre, up_pre)
    grad_gate_pre, grad_up_pre = act_pull(grad_hidden)
    grad_gate_pre = grad_gate_pre.astype(jnp.bfloat16)
    grad_up_pre = grad_up_pre.astype(jnp.bfloat16)
    grad_gate = jnp.dot(second_normed.T.astype(jnp.float32), grad_gate_pre.astype(jnp.float32), preferred_element_type=jnp.float32)
    grad_up = jnp.dot(second_normed.T.astype(jnp.float32), grad_up_pre.astype(jnp.float32), preferred_element_type=jnp.float32)
    grad_normed_two = jnp.dot(grad_gate_pre.astype(jnp.float32), weight_gate.T.astype(jnp.float32), preferred_element_type=jnp.float32) + jnp.dot(grad_up_pre.astype(jnp.float32), weight_up.T.astype(jnp.float32), preferred_element_type=jnp.float32)
    _, norm_pull = jax.vjp(rms_norm, stream_mid, gain_two)
    grad_mid, grad_gain_two = norm_pull(grad_normed_two)
    grad_stream = grad_stream + grad_mid
    back_bf = grad_stream.astype(jnp.bfloat16)
    grad_out = jnp.dot(gated_out.T.astype(jnp.float32), back_bf.astype(jnp.float32), preferred_element_type=jnp.float32)
    grad_gated = jnp.dot(back_bf.astype(jnp.float32), weight_out.T.astype(jnp.float32), preferred_element_type=jnp.float32).reshape(length_total, -1, DV)
    _, post_pull = jax.vjp(post_mix, outputs, gate_z, out_gain)
    grad_outputs, grad_gate_z, grad_out_gain = post_pull(grad_gated)
    zero_state = jnp.zeros((H, DV, DK), jnp.float32)

    def core_only(queries, keys_unit, values_in):
        return delta_rule(queries, keys_unit, values_in, logdecay, beta_rate, zero_state)[0]
    _, rule_pull = jax.vjp(core_only, queries, keys_unit, values_in)
    grad_queries, grad_keys, grad_values = rule_pull(grad_outputs)
    _, mix_pull = jax.vjp(mixer_inputs, windowed, conv_taps)
    grad_window, grad_conv = mix_pull((grad_queries, grad_keys, grad_values))
    grad_conv_in = grad_window[CONV - 1:]
    grad_proj = jnp.concatenate([grad_conv_in.reshape(length_total, -1, 2 * DK + DV), grad_gate_z], axis=2).reshape(length_total, -1).astype(jnp.bfloat16)
    grad_in = jnp.dot(normed.T.astype(jnp.float32), grad_proj.astype(jnp.float32), preferred_element_type=jnp.float32)
    grad_normed = jnp.dot(grad_proj.astype(jnp.float32), weight_in.T.astype(jnp.float32), preferred_element_type=jnp.float32)
    _, norm_pull = jax.vjp(rms_norm, stream, gain_one)
    grad_prev, grad_gain_one = norm_pull(grad_normed)
    return (grad_stream + grad_prev, (grad_gain_one, grad_in, grad_conv, grad_out_gain, grad_out, grad_gain_two, grad_gate, grad_up, grad_down))

def reference(tokens, cotangent, gate_code, beta_code, norm1_gain, weight_in, conv_weight, out_gain, weight_out, norm2_gain, weight_gate, weight_up, weight_down):
    logdecay = -gate_code.astype(jnp.float32) * gate_unit
    beta_rate = beta_code.astype(jnp.float32) * beta_unit
    everything = (norm1_gain, weight_in, conv_weight, out_gain, weight_out, norm2_gain, weight_gate, weight_up, weight_down)
    stream = tokens.astype(jnp.float32)
    kept_layers = []
    for layer_idx in range(STACK_LEVELS):
        weights = tuple((tensor[layer_idx] for tensor in everything))
        stream, stored = layer_forward(stream, logdecay[layer_idx], beta_rate[layer_idx], weights)
        kept_layers.append((weights, stored))
    activations = stream.astype(jnp.bfloat16)
    grad_stream = cotangent.astype(jnp.float32)
    ordered = []
    for layer_idx in reversed(range(STACK_LEVELS)):
        weights, stored = kept_layers[layer_idx]
        grad_stream, layer_grads = layer_backward(grad_stream, logdecay[layer_idx], beta_rate[layer_idx], weights, stored)
        ordered.insert(0, layer_grads)
    stacked = [jnp.stack([grad_group[slot_index] for grad_group in ordered]) for slot_index in range(9)]
    return (activations, grad_stream, stacked[0], stacked[1], stacked[2], stacked[3], stacked[4], stacked[5], stacked[6], stacked[7], stacked[8])
```

```python
import functools

import jax
import jax.numpy as jnp
from jax import lax
from jax.experimental import pallas as pl
from jax.experimental.pallas import tpu as pltpu
from jax.sharding import PartitionSpec as P

DK = 128
DV = 256
CONV = 4
STACK_LEVELS = 2
QKV = 2 * DK + DV
WIDE = 2 * DK + 2 * DV
HALF = DV // 2
PAD = 8

f32 = jnp.float32
bf16 = jnp.bfloat16
highest = lax.Precision.HIGHEST
norm_eps = 1e-06
gate_unit = 1.0 / 1048576.0
beta_unit = 1.0 / 1024.0


def shape_of(dims, dtype=f32):
    return jax.ShapeDtypeStruct(tuple(dims), dtype)


def call(body, outs, args, name, scratch=()):
    specs = []
    for arg in args:
        if arg.dtype == jnp.int32:
            specs.append(pl.BlockSpec(memory_space=pltpu.SMEM))
        else:
            specs.append(pl.BlockSpec(memory_space=pltpu.VMEM))
    return pl.pallas_call(
        body,
        out_shape=tuple(outs),
        in_specs=specs,
        out_specs=tuple(pl.BlockSpec(memory_space=pltpu.VMEM) for _ in outs),
        scratch_shapes=list(scratch),
        name=name,
    )(*args)


def mm(a, b, ca, cb, precision=highest):
    return lax.dot_general(
        a, b, (((ca,), (cb,)), ((), ())), precision=precision, preferred_element_type=f32
    )


def mmb(a, b, ca, cb):
    return lax.dot_general(
        a.astype(bf16), b.astype(bf16), (((ca,), (cb,)), ((), ())), preferred_element_type=f32
    )


def sigmoid(u):
    return 1.0 / (1.0 + jnp.exp(-u))


def norm_forward(x, gain):
    return x * lax.rsqrt(jnp.mean(x * x, axis=-1, keepdims=True) + norm_eps) * gain


def norm_backward(x, gain, grad):
    rate = lax.rsqrt(jnp.mean(x * x, axis=-1, keepdims=True) + norm_eps)
    unit = x * rate
    grad_gain = jnp.sum(grad * unit, axis=0, keepdims=True)
    scaled = grad * gain
    grad_x = rate * (scaled - unit * jnp.mean(scaled * unit, axis=-1, keepdims=True))
    return grad_x, grad_gain


def in_kernel(stream_ref, gain_ref, w_ref, normed_ref, proj_ref):
    normed = norm_forward(stream_ref[...], gain_ref[...]).astype(bf16)
    normed_ref[...] = normed
    proj_ref[...] = mmb(normed, w_ref[...], 1, 0)


def in_sum_kernel(mid_ref, total_ref, gain_ref, w_ref, stream_ref, normed_ref, proj_ref):
    stream = mid_ref[...] + total_ref[...]
    stream_ref[...] = stream
    normed = norm_forward(stream, gain_ref[...]).astype(bf16)
    normed_ref[...] = normed
    proj_ref[...] = mmb(normed, w_ref[...], 1, 0)


def conv_of(win_ref, taps, length):
    conv = taps[0:1] * win_ref[pl.ds(PAD, length), :]
    for tap in range(1, CONV):
        conv = conv + taps[tap : tap + 1] * win_ref[pl.ds(PAD - tap, length), :]
    return conv


def decay_of(col, row, length):
    rows = lax.broadcasted_iota(jnp.int32, (length, length), 0)
    cols = lax.broadcasted_iota(jnp.int32, (length, length), 1)
    keep = rows >= cols
    ratio = jnp.where(keep, jnp.exp(jnp.where(keep, col - row, 0.0)), 0.0)
    return rows, cols, ratio


def delta_kernel(
    y_ref, proj_ref, before_ref, taps_ref, col_ref, row_ref, beta_ref,
    ow_ref, uw_ref, solve_ref, mix_ref, send_ref, keep_ref, transfer_ref,
    win_ref, offset_ref,
):
    length = proj_ref.shape[0]
    for head in range(col_ref.shape[0]):
        base = head * WIDE
        win_ref[0:PAD, :] = before_ref[:, base : base + QKV]
        win_ref[pl.ds(PAD, length), :] = proj_ref[:, base : base + QKV]
        conv = conv_of(win_ref, taps_ref[:, head * QKV : (head + 1) * QKV].astype(f32), length)
        active = conv * sigmoid(conv)
        q_act = active[:, :DK]
        k_act = active[:, DK : 2 * DK]
        values = active[:, 2 * DK :]
        q = q_act * lax.rsqrt(jnp.sum(q_act * q_act, axis=-1, keepdims=True) + norm_eps)
        q = q * DK ** (-0.5)
        k = k_act * lax.rsqrt(jnp.sum(k_act * k_act, axis=-1, keepdims=True) + norm_eps)
        col = col_ref[head]
        row = row_ref[head]
        beta = beta_ref[head]
        rows, cols, ratio = decay_of(col, row, length)
        key_key = mm(k, k, 1, 1)
        query_key = mm(q, k, 1, 1)
        lower = jnp.where(rows > cols, beta * ratio * key_key, 0.0)
        solve = jnp.where(rows == cols, 1.0, 0.0)
        block = 1
        while block < length:
            here = (
                (rows // (2 * block) == cols // (2 * block))
                & (rows % (2 * block) >= block)
                & (cols % (2 * block) < block)
            )
            part = jnp.where(here, lower, 0.0)
            if block == 1:
                solve = solve - part
            else:
                solve = solve - mm(solve, mm(part, solve, 1, 0), 1, 0)
            block *= 2
        decay = jnp.exp(col)
        right = jnp.concatenate([beta * values, (beta * decay) * k], axis=1)
        uw = mm(solve, right, 1, 0)
        mix = ratio * query_key
        muw = mm(mix, uw, 1, 0)
        last = row[:, length - 1 :]
        ends = mm(uw, jnp.exp(last - col) * k, 0, 0)
        eye = jnp.where(
            lax.broadcasted_iota(jnp.int32, (DK, DK), 0)
            == lax.broadcasted_iota(jnp.int32, (DK, DK), 1),
            1.0,
            0.0,
        )
        transfer = jnp.exp(last) * eye - ends[DV:]
        offset_ref[...] = ends[:DV]
        ow_ref[head] = jnp.concatenate([muw[:, :DV], decay * q - muw[:, DV:]], axis=1)
        uw_ref[head] = uw
        solve_ref[head] = solve
        mix_ref[head] = mix
        transfer_ref[head] = transfer
        y = y_ref[0]
        send_ref[head, 0:DK, :] = transfer
        send_ref[head, DK : DK + HALF, :] = offset_ref[
            pl.ds(pl.multiple_of((1 - y) * HALF, HALF), HALF), :
        ]
        keep_ref[head] = offset_ref[pl.ds(pl.multiple_of(y * HALF, HALF), HALF), :]


def pair_kernel(
    y_ref, own_ref, keep_ref, other_ref,
    first_t_ref, second_t_ref, pair_t_ref, first_o_ref, pair_o_ref,
):
    lead = y_ref[0] == 0
    for head in range(own_ref.shape[0]):
        own, other = own_ref[head], other_ref[head, 0:DK, :]
        keep, far = keep_ref[head], other_ref[head, DK : DK + HALF, :]
        first_t, second_t = jnp.where(lead, own, other), jnp.where(lead, other, own)
        first_o, second_o = jnp.where(lead, keep, far), jnp.where(lead, far, keep)
        first_t_ref[head] = first_t
        second_t_ref[head] = second_t
        first_o_ref[head] = first_o
        both = mm(jnp.concatenate([first_t, first_o], axis=0), second_t, 1, 0)
        pair_t_ref[head] = both[:DK]
        pair_o_ref[head] = both[DK:] + second_o


def step_kernel(state_ref, transfer_ref, offset_ref, out_ref):
    for head in range(state_ref.shape[0]):
        out_ref[head] = mm(state_ref[head], transfer_ref[head], 1, 0) + offset_ref[head]


def step_back_kernel(state_ref, transfer_ref, offset_ref, out_ref):
    for head in range(state_ref.shape[0]):
        out_ref[head] = mm(state_ref[head], transfer_ref[head], 1, 1) + offset_ref[head]


def last_kernel(y_ref, state_ref, transfer_ref, offset_ref, mine_ref, other_ref):
    lead = y_ref[0] == 0
    for head in range(state_ref.shape[0]):
        state = state_ref[head]
        moved = mm(state, transfer_ref[head], 1, 0) + offset_ref[head]
        mine_ref[head] = jnp.where(lead, state, moved)
        other_ref[head] = jnp.where(lead, moved, state)


def pair_back_kernel(y_ref, keep_ref, other_ref, first_t_ref, second_ref, pair_ref):
    lead = y_ref[0] == 0
    for head in range(keep_ref.shape[0]):
        keep, far = keep_ref[head], other_ref[head]
        first, second = jnp.where(lead, keep, far), jnp.where(lead, far, keep)
        second_ref[head] = second
        pair_ref[head] = first + mm(second, first_t_ref[head], 1, 1)


def last_back_kernel(y_ref, state_ref, transfer_ref, offset_ref, mine_ref, other_ref):
    lead = y_ref[0] == 0
    for head in range(state_ref.shape[0]):
        state = state_ref[head]
        moved = mm(state, transfer_ref[head], 1, 1) + offset_ref[head]
        mine_ref[head] = jnp.where(lead, moved, state)
        other_ref[head] = jnp.where(lead, state, moved)


def halves(y, mine, other):
    lead = y == 0
    return jnp.concatenate(
        [jnp.where(lead, mine, other), jnp.where(lead, other, mine)], axis=0
    )


def out_kernel(
    y_ref, mine_ref, other_ref, ow_ref, proj_ref, gain_ref, w_ref,
    state_ref, outputs_ref, gated_ref, part_ref,
):
    pieces = []
    for head in range(ow_ref.shape[0]):
        state = halves(y_ref[0], mine_ref[head], other_ref[head])
        state_ref[head] = state
        ow = ow_ref[head]
        outputs = ow[:, :DV] + mm(ow[:, DV:], state, 1, 1)
        outputs_ref[:, head * DV : (head + 1) * DV] = outputs
        z = proj_ref[:, head * WIDE + QKV : (head + 1) * WIDE]
        pieces.append((norm_forward(outputs, gain_ref[...]) * (z * sigmoid(z))).astype(bf16))
    gated = jnp.concatenate(pieces, axis=1)
    gated_ref[...] = gated
    part_ref[...] = mmb(gated, w_ref[...], 1, 0)


def ffn_kernel(
    stream_ref, total_ref, gain_ref, wg_ref, wu_ref, wd_ref,
    mid_ref, normed_ref, gate_ref, up_ref, hidden_ref, part_ref,
):
    mid = stream_ref[...] + total_ref[...]
    mid_ref[...] = mid
    normed = norm_forward(mid, gain_ref[...]).astype(bf16)
    normed_ref[...] = normed
    gate = mmb(normed, wg_ref[...], 1, 0)
    up = mmb(normed, wu_ref[...], 1, 0)
    gate_ref[...] = gate
    up_ref[...] = up
    hidden = (gate * sigmoid(gate) * up).astype(bf16)
    hidden_ref[...] = hidden
    part_ref[...] = mmb(hidden, wd_ref[...], 1, 0)


def sum_kernel(mid_ref, total_ref, out_ref):
    out_ref[...] = (mid_ref[...] + total_ref[...]).astype(bf16)


def ffn_back_kernel(
    grad_ref, gate_ref, up_ref, wg_ref, wu_ref, wd_ref,
    back_ref, gg_ref, gu_ref, part_ref,
):
    back = grad_ref[...].astype(bf16)
    back_ref[...] = back.astype(f32)
    hidden = mmb(back, wd_ref[...], 1, 1)
    gate, up = gate_ref[...], up_ref[...]
    rate = sigmoid(gate)
    gu = (hidden * (gate * rate)).astype(bf16)
    gg = (hidden * up * (rate * (1.0 + gate * (1.0 - rate)))).astype(bf16)
    gg_ref[...] = gg.astype(f32)
    gu_ref[...] = gu.astype(f32)
    part_ref[...] = mmb(gg, wg_ref[...], 1, 1) + mmb(gu, wu_ref[...], 1, 1)


def out_back_kernel(
    y_ref, grad_ref, total_ref, mid_ref, gain_ref, w_ref, outputs_ref, proj_ref, out_gain_ref,
    ow_ref,
    next_ref, back_ref, do_ref, dz_ref, dgain_ref, dout_gain_ref, send_ref, keep_ref,
    local_ref,
):
    grad_mid, grad_gain = norm_backward(mid_ref[...], gain_ref[...], total_ref[...])
    dgain_ref[...] = grad_gain
    grad = grad_ref[...] + grad_mid
    next_ref[...] = grad
    back = grad.astype(bf16)
    back_ref[...] = back.astype(f32)
    gated = mmb(back, w_ref[...], 1, 1)
    gain = out_gain_ref[...]
    total_gain = jnp.zeros_like(gain)
    y = y_ref[0]
    for head in range(ow_ref.shape[0]):
        span = slice(head * DV, (head + 1) * DV)
        outputs = outputs_ref[:, span]
        z = proj_ref[:, head * WIDE + QKV : (head + 1) * WIDE]
        rate = sigmoid(z)
        grad_h = gated[:, span]
        grad_n = grad_h * (z * rate)
        dz_ref[:, span] = (
            grad_h * norm_forward(outputs, gain) * (rate * (1.0 + z * (1.0 - rate)))
        )
        grad_o, gain_part = norm_backward(outputs, gain, grad_n)
        total_gain = total_gain + gain_part
        do_ref[:, span] = grad_o
        local_ref[...] = mm(grad_o, ow_ref[head][:, DV:], 0, 0)
        send_ref[head] = local_ref[pl.ds(pl.multiple_of((1 - y) * HALF, HALF), HALF), :]
        keep_ref[head] = local_ref[pl.ds(pl.multiple_of(y * HALF, HALF), HALF), :]
    dout_gain_ref[...] = total_gain


def delta_back_kernel(
    y_ref, mine_ref, other_ref, state_ref, uw_ref, solve_ref, mix_ref, do_ref,
    proj_ref, before_ref, taps_ref, col_ref, row_ref, beta_ref,
    dconv_ref, dtaps_ref, edge_ref,
    win_ref,
):
    length = proj_ref.shape[0]
    for head in range(col_ref.shape[0]):
        base = head * WIDE
        win_ref[0:PAD, :] = before_ref[:, base : base + QKV]
        win_ref[pl.ds(PAD, length), :] = proj_ref[:, base : base + QKV]
        taps = taps_ref[:, head * QKV : (head + 1) * QKV].astype(f32)
        conv = conv_of(win_ref, taps, length)
        rate = sigmoid(conv)
        active = conv * rate
        q_act = active[:, :DK]
        k_act = active[:, DK : 2 * DK]
        q_rate = lax.rsqrt(jnp.sum(q_act * q_act, axis=-1, keepdims=True) + norm_eps)
        k_rate = lax.rsqrt(jnp.sum(k_act * k_act, axis=-1, keepdims=True) + norm_eps)
        q_unit = q_act * q_rate
        k = k_act * k_rate
        q = q_unit * DK ** (-0.5)
        col = col_ref[head]
        row = row_ref[head]
        beta = beta_ref[head]
        rows, cols, ratio = decay_of(col, row, length)
        decay = jnp.exp(col)
        to_end = jnp.exp(row[:, length - 1 :] - col)
        state = state_ref[head]
        grad_end = halves(y_ref[0], mine_ref[head], other_ref[head])
        uw = uw_ref[head]
        grad_o = do_ref[:, head * DV : (head + 1) * DV]
        values_new = uw[:, :DV] - mm(uw[:, DV:], state, 1, 1)
        grad_new = mm(mix_ref[head], grad_o, 0, 0) + mm(to_end * k, grad_end, 1, 1)
        grad_right = mm(solve_ref[head], grad_new, 0, 0)
        grad_mix = jnp.where(rows >= cols, ratio * mm(grad_o, values_new, 1, 1), 0.0)
        grad_low = jnp.where(
            rows > cols, -(beta * ratio) * mm(grad_right, values_new, 1, 1), 0.0
        )
        grad_q = decay * mm(grad_o, state, 1, 0) + mm(grad_mix, k, 1, 0)
        grad_k = to_end * mm(values_new, grad_end, 1, 0)
        grad_k = grad_k - (beta * decay) * mm(grad_right, state, 1, 0)
        grad_k = grad_k + mm(grad_low, k, 1, 0) + mm(grad_low, k, 0, 0)
        grad_k = grad_k + mm(grad_mix, q, 0, 0)
        grad_v = beta * grad_right
        grad_qa = (DK ** (-0.5)) * q_rate * (
            grad_q - q_unit * jnp.sum(grad_q * q_unit, axis=-1, keepdims=True)
        )
        grad_ka = k_rate * (grad_k - k * jnp.sum(grad_k * k, axis=-1, keepdims=True))
        grad_conv = jnp.concatenate([grad_qa, grad_ka, grad_v], axis=1) * (
            rate * (1.0 + conv * (1.0 - rate))
        )
        span = slice(head * QKV, (head + 1) * QKV)
        dconv_ref[:, span] = grad_conv
        edge_ref[:, span] = grad_conv[0:PAD]
        for tap in range(CONV):
            dtaps_ref[tap : tap + 1, span] = jnp.sum(
                grad_conv * win_ref[pl.ds(PAD - tap, length), :], axis=0, keepdims=True
            )


def in_back_kernel(
    dconv_ref, after_ref, taps_ref, dz_ref, w_ref, gp_ref, part_ref, ext_ref
):
    length = dconv_ref.shape[0]
    ext_ref[pl.ds(0, length), :] = dconv_ref[...]
    ext_ref[pl.ds(length, PAD), :] = after_ref[...]
    taps = taps_ref[...].astype(f32)
    total = taps[0:1] * ext_ref[pl.ds(0, length), :]
    for tap in range(1, CONV):
        total = total + taps[tap : tap + 1] * ext_ref[pl.ds(tap, length), :]
    pieces = []
    for head in range(total.shape[1] // QKV):
        pieces.append(total[:, head * QKV : (head + 1) * QKV])
        pieces.append(dz_ref[:, head * DV : (head + 1) * DV])
    grad_proj = jnp.concatenate(pieces, axis=1).astype(bf16)
    gp_ref[...] = grad_proj.astype(f32)
    part_ref[...] = mmb(grad_proj, w_ref[...], 1, 1)


def norm_back_kernel(grad_ref, total_ref, stream_ref, gain_ref, out_ref, dgain_ref):
    grad_x, grad_gain = norm_backward(stream_ref[...], gain_ref[...], total_ref[...])
    out_ref[...] = grad_ref[...] + grad_x
    dgain_ref[...] = grad_gain


def weight_kernel(*refs, widths):
    out_ref = refs[-1]
    start = 0
    for index, width in enumerate(widths):
        a, b, a_far, b_far = refs[4 * index : 4 * index + 4]
        out_ref[:, start : start + width] = mmb(a[...], b[...], 0, 0) + mmb(
            a_far[...], b_far[...], 0, 0
        )
        start += width


def shift(array, axis, by):
    length = lax.axis_size(axis)
    pairs = [(i, i + by) for i in range(length) if 0 <= i + by < length]
    return lax.ppermute(array, axis, pairs)


def swap(array, axis, bit):
    length = lax.axis_size(axis)
    return lax.ppermute(array, axis, [(i, i ^ bit) for i in range(length)])


def head_total(part):
    size = lax.axis_size("head")
    rows = part.shape[0] // 2
    bit = lax.axis_index("head") % 2
    mine = lax.dynamic_slice_in_dim(part, bit * rows, rows, 0)
    other = lax.dynamic_slice_in_dim(part, (1 - bit) * rows, rows, 0)
    total = mine + swap(other, "head", 1)
    step = 2
    while step < size:
        total = total + swap(total, "head", step)
        step *= 2
    far = swap(total, "head", 1)
    return jnp.where(
        bit == 0, jnp.concatenate([total, far], 0), jnp.concatenate([far, total], 0)
    )


def full_sum(array, axis):
    step = 1
    while step < lax.axis_size(axis):
        array = array + swap(array, axis, step)
        step *= 2
    return array


def blocks_of(array, parity):
    size = lax.axis_size("seq")
    length, width = array.shape
    parts = array.reshape(length, size // 2, 2, width // size)
    return lax.dynamic_index_in_dim(parts, parity, 2, keepdims=False).reshape(length, width // 2)


def outer_scatter(array):
    size = lax.axis_size("seq")
    groups = [[2 * o + p for o in range(size // 2)] for p in range(2)]
    return lax.psum_scatter(
        array, "seq", scatter_dimension=0, tiled=True, axis_index_groups=groups
    )


def layer_forward(start, col, row, beta, weights, y):
    gain_one, w_in, taps, out_gain, w_out, gain_two, w_gate, w_up, w_down = weights
    length, width = start[0].shape
    heads = col.shape[0]
    proj_width = w_in.shape[1]
    if len(start) == 1:
        stream = start[0]
        normed, proj = call(
            in_kernel,
            [shape_of((length, width), bf16), shape_of((length, proj_width))],
            [stream, gain_one, w_in],
            "in_proj",
        )
    else:
        stream, normed, proj = call(
            in_sum_kernel,
            [
                shape_of((length, width)),
                shape_of((length, width), bf16),
                shape_of((length, proj_width)),
            ],
            [start[0], start[1], gain_one, w_in],
            "in_proj_sum",
        )
    before = shift(proj[length - PAD :], "seq", 1)
    square = shape_of((heads, DK, DK))
    wide = shape_of((heads, length, DV + DK))
    inner = shape_of((heads, length, length))
    half = shape_of((heads, HALF, DK))
    ow, uw, solve, mix, send, keep, transfer = call(
        delta_kernel,
        [wide, wide, inner, inner, shape_of((heads, DK + HALF, DK)), half, square],
        [y, proj, before, taps, col, row, beta],
        "delta",
        [pltpu.VMEM((length + PAD, QKV), f32), pltpu.VMEM((DV, DK), f32)],
    )
    far = swap(send, "seq", 1)
    first_t, second_t, pair_t, first_o, pair_o = call(
        pair_kernel, [square, square, square, half, half], [y, transfer, keep, far], "pair"
    )
    outer = lax.axis_size("seq") // 2
    state = shift(pair_o, "seq", 2)
    for _ in range(outer - 2):
        (moved,) = call(step_kernel, [half], [state, pair_t, pair_o], "step")
        state = shift(moved, "seq", 2)
    mine, other = call(last_kernel, [half, half], [y, state, first_t, first_o], "last")
    other = swap(other, "seq", 1)
    incoming, outputs, gated, part = call(
        out_kernel,
        [
            shape_of((heads, DV, DK)),
            shape_of((length, heads * DV)),
            shape_of((length, heads * DV), bf16),
            shape_of((length, width)),
        ],
        [y, mine, other, ow, proj, out_gain, w_out],
        "out_proj",
    )
    total = head_total(part)
    hidden_width = w_gate.shape[1]
    mid, normed_two, gate, up, hidden, part = call(
        ffn_kernel,
        [
            shape_of((length, width)),
            shape_of((length, width), bf16),
            shape_of((length, hidden_width)),
            shape_of((length, hidden_width)),
            shape_of((length, hidden_width), bf16),
            shape_of((length, width)),
        ],
        [stream, total, gain_two, w_gate, w_up, w_down],
        "ffn",
    )
    total = head_total(part)
    parity = lax.axis_index("seq") % 2
    sent = jnp.concatenate(
        [
            blocks_of(normed, 1 - parity).astype(f32),
            gated.astype(f32),
            blocks_of(normed_two, 1 - parity).astype(f32),
            hidden.astype(f32),
        ],
        axis=1,
    )
    far_forward = swap(sent, "seq", 1)
    stored = dict(
        stream=stream, normed=normed, proj=proj, before=before, ow=ow, uw=uw, solve=solve,
        mix=mix, first_t=first_t, second_t=second_t, pair_t=pair_t, incoming=incoming,
        outputs=outputs, gated=gated, mid=mid, normed_two=normed_two, gate=gate, up=up,
        hidden=hidden, far_forward=far_forward,
    )
    return (mid, total), stored


def layer_backward(grad, col, row, beta, weights, kept, y):
    gain_one, w_in, taps, out_gain, w_out, gain_two, w_gate, w_up, w_down = weights
    length, width = grad.shape
    heads = col.shape[0]
    hidden_width = w_gate.shape[1]
    proj_width = w_in.shape[1]
    parity = lax.axis_index("seq") % 2
    half_width = width // 2
    back, gg, gu, part = call(
        ffn_back_kernel,
        [
            shape_of((length, width)),
            shape_of((length, hidden_width)),
            shape_of((length, hidden_width)),
            shape_of((length, width)),
        ],
        [grad, kept["gate"], kept["up"], w_gate, w_up, w_down],
        "ffn_back",
    )
    total = head_total(part)
    far_forward = kept["far_forward"]
    value_width = heads * DV
    normed_far = far_forward[:, :half_width]
    gated_far = far_forward[:, half_width : half_width + value_width]
    normed_two_far = far_forward[
        :, half_width + value_width : 2 * half_width + value_width
    ]
    hidden_far = far_forward[:, 2 * half_width + value_width :]
    far_ffn = swap(
        jnp.concatenate([gg, gu, blocks_of(back, 1 - parity)], axis=1), "seq", 1
    )
    both = 2 * hidden_width
    (ffn_weights,) = call(
        functools.partial(weight_kernel, widths=(both, hidden_width)),
        [shape_of((half_width, both + hidden_width))],
        [
            blocks_of(kept["normed_two"], parity),
            jnp.concatenate([gg, gu], axis=1),
            normed_two_far,
            far_ffn[:, :both],
            blocks_of(back, parity),
            kept["hidden"],
            far_ffn[:, both:],
            hidden_far,
        ],
        "weights_ffn",
    )
    ffn_weights = outer_scatter(ffn_weights)
    half = shape_of((heads, HALF, DK))
    grad, back, grad_o, grad_z, dgain_two, dout_gain, send, keep = call(
        out_back_kernel,
        [
            shape_of((length, width)),
            shape_of((length, width)),
            shape_of((length, value_width)),
            shape_of((length, value_width)),
            shape_of((1, width)),
            shape_of((1, DV)),
            half,
            half,
        ],
        [
            y, grad, total, kept["mid"], gain_two, w_out, kept["outputs"], kept["proj"], out_gain,
            kept["ow"],
        ],
        "out_back",
        [pltpu.VMEM((DV, DK), f32)],
    )
    far = swap(send, "seq", 1)
    second_o, pair_o = call(
        pair_back_kernel, [half, half], [y, keep, far, kept["first_t"]], "pair_back"
    )
    outer = lax.axis_size("seq") // 2
    state = shift(pair_o, "seq", -2)
    for _ in range(outer - 2):
        (moved,) = call(step_back_kernel, [half], [state, kept["pair_t"], pair_o], "step_back")
        state = shift(moved, "seq", -2)
    mine, other = call(
        last_back_kernel, [half, half], [y, state, kept["second_t"], second_o], "last_back"
    )
    other = swap(other, "seq", 1)
    qkv_width = heads * QKV
    dconv, dtaps, edge = call(
        delta_back_kernel,
        [
            shape_of((length, qkv_width)),
            shape_of((CONV, qkv_width)),
            shape_of((PAD, qkv_width)),
        ],
        [
            y, mine, other, kept["incoming"], kept["uw"], kept["solve"], kept["mix"], grad_o,
            kept["proj"], kept["before"], taps, col, row, beta,
        ],
        "delta_back",
        [pltpu.VMEM((length + PAD, QKV), f32)],
    )
    after = shift(edge, "seq", -1)
    grad_proj, part = call(
        in_back_kernel,
        [shape_of((length, proj_width)), shape_of((length, width))],
        [dconv, after, taps, grad_z, w_in],
        "in_back",
        [pltpu.VMEM((length + PAD, qkv_width), f32)],
    )
    far_mix = swap(
        jnp.concatenate([grad_proj, blocks_of(back, 1 - parity)], axis=1), "seq", 1
    )
    (mix_weights,) = call(
        functools.partial(weight_kernel, widths=(proj_width, value_width)),
        [shape_of((half_width, proj_width + value_width))],
        [
            blocks_of(kept["normed"], parity),
            grad_proj,
            normed_far,
            far_mix[:, :proj_width],
            blocks_of(back, parity),
            kept["gated"],
            far_mix[:, proj_width:],
            gated_far,
        ],
        "weights_mix",
    )
    mix_weights = outer_scatter(mix_weights)
    total = head_total(part)
    grad, dgain_one = call(
        norm_back_kernel,
        [shape_of((length, width)), shape_of((1, width))],
        [grad, total, kept["stream"], gain_one],
        "norm_back",
    )
    return grad, (ffn_weights, mix_weights, dtaps, dgain_one, dout_gain, dgain_two)


def body(
    tokens,
    cotangent,
    gate_code,
    beta_code,
    norm1_gain,
    weight_in,
    conv_weight,
    out_gain,
    weight_out,
    norm2_gain,
    weight_gate,
    weight_up,
    weight_down,
):
    y = (lax.axis_index("seq") % 2).astype(jnp.int32).reshape(1)
    logdecay = -gate_code.astype(f32) * gate_unit
    beta_rate = beta_code.astype(f32) * beta_unit
    cumulated = jnp.transpose(jnp.cumsum(logdecay, axis=1), (0, 2, 1))
    beta_rate = jnp.transpose(beta_rate, (0, 2, 1))
    layers = []
    for level in range(STACK_LEVELS):
        layers.append(
            (
                cumulated[level][:, :, None],
                cumulated[level][:, None, :],
                beta_rate[level][:, :, None],
                (
                    norm1_gain[level][None],
                    weight_in[level],
                    conv_weight[level],
                    out_gain[level][None],
                    weight_out[level],
                    norm2_gain[level][None],
                    weight_gate[level],
                    weight_up[level],
                    weight_down[level],
                ),
            )
        )
    start = (tokens.astype(f32),)
    kept = []
    for level in range(STACK_LEVELS):
        start, stored = layer_forward(start, *layers[level], y)
        kept.append(stored)
    (activations,) = call(sum_kernel, [shape_of(tokens.shape, bf16)], list(start), "finish")
    grad = cotangent.astype(f32)
    parts = [None] * STACK_LEVELS
    for level in reversed(range(STACK_LEVELS)):
        grad, parts[level] = layer_backward(grad, *layers[level], kept[level], y)
    hidden_width = weight_gate.shape[2]
    proj_width = weight_in.shape[2]
    ffn = jnp.stack([part[0] for part in parts])
    mixer = jnp.stack([part[1] for part in parts])
    grad_gate = ffn[:, :, :hidden_width]
    grad_up = ffn[:, :, hidden_width : 2 * hidden_width]
    grad_down = jnp.transpose(ffn[:, :, 2 * hidden_width :], (0, 2, 1))
    grad_in = mixer[:, :, :proj_width]
    grad_out = jnp.transpose(mixer[:, :, proj_width:], (0, 2, 1))
    qkv_width = conv_weight.shape[2]
    width = tokens.shape[1]
    out_gain_part = full_sum(jnp.concatenate([part[4] for part in parts], axis=0), "head")
    small = jnp.concatenate(
        [part[2].reshape(1, -1) for part in parts]
        + [part[3] for part in parts]
        + [part[5] for part in parts]
        + [out_gain_part.reshape(1, -1)],
        axis=1,
    )
    small = full_sum(small, "seq")[0]
    sizes = [STACK_LEVELS * CONV * qkv_width, STACK_LEVELS * width, STACK_LEVELS * width]
    conv_grad = small[: sizes[0]].reshape(STACK_LEVELS, CONV, qkv_width)
    gain_one_grad = small[sizes[0] : sizes[0] + sizes[1]].reshape(STACK_LEVELS, width)
    gain_two_grad = small[sizes[0] + sizes[1] : sum(sizes)].reshape(STACK_LEVELS, width)
    out_gain_grad = small[sum(sizes) :].reshape(STACK_LEVELS, DV)
    return (
        activations,
        grad,
        gain_one_grad,
        grad_in,
        conv_grad,
        out_gain_grad,
        grad_out,
        gain_two_grad,
        grad_gate,
        grad_up,
        grad_down,
    )


def solution(mesh):
    in_specs = (
        P("seq", None),
        P("seq", None),
        P(None, "seq", "head"),
        P(None, "seq", "head"),
        P(),
        P(None, None, "head"),
        P(None, None, "head"),
        P(),
        P(None, "head", None),
        P(),
        P(None, None, "head"),
        P(None, None, "head"),
        P(None, "head", None),
    )
    out_specs = (
        P("seq", None),
        P("seq", None),
        P(),
        P(None, "seq", "head"),
        P(None, None, "head"),
        P(),
        P(None, "head", "seq"),
        P(),
        P(None, "seq", "head"),
        P(None, "seq", "head"),
        P(None, "head", "seq"),
    )
    return jax.shard_map(body, mesh=mesh, in_specs=in_specs, out_specs=out_specs, check_vma=False)
```

```python
import functools

import jax
import jax.numpy as jnp
from jax import lax
from jax.experimental import pallas as pl
from jax.experimental.pallas import tpu as pltpu
from jax.sharding import PartitionSpec as P

DK = 128
DV = 256
CONV = 4
STACK_LEVELS = 2
QKV = 2 * DK + DV
WIDE = 2 * DK + 2 * DV
HALF = DV // 2
PAD = 8

f32 = jnp.float32
bf16 = jnp.bfloat16
norm_eps = 1e-06
gate_unit = 1.0 / 1048576.0
beta_unit = 1.0 / 1024.0


def shape_of(dims, dtype=f32):
    return jax.ShapeDtypeStruct(tuple(dims), dtype)


def call(body, outs, args, name, scratch=()):
    specs, arrays = [], []
    for arg in args:
        if isinstance(arg, tuple):
            array, level = arg
            rest = (0,) * (array.ndim - 1)
            specs.append(
                pl.BlockSpec((None,) + array.shape[1:], functools.partial(at_level, level, rest))
            )
        elif arg.dtype == jnp.int32:
            array = arg
            specs.append(pl.BlockSpec(memory_space=pltpu.SMEM))
        else:
            array = arg
            specs.append(pl.BlockSpec(memory_space=pltpu.VMEM))
        arrays.append(array)
    with jax.named_scope("k_" + name):
        return pl.pallas_call(
            body,
            grid=(1,),
            out_shape=tuple(outs),
            in_specs=specs,
            out_specs=tuple(pl.BlockSpec(memory_space=pltpu.VMEM) for _ in outs),
            scratch_shapes=list(scratch),
            name=name,
        )(*arrays)


def at_level(level, rest, _):
    return (level,) + rest


def mm(a, b, ca, cb):
    a_high, b_high = a.astype(bf16), b.astype(bf16)
    a_low = (a - a_high.astype(f32)).astype(bf16)
    b_low = (b - b_high.astype(f32)).astype(bf16)
    return mmb(a_high, b_high, ca, cb) + (mmb(a_high, b_low, ca, cb) + mmb(a_low, b_high, ca, cb))


def mmb(a, b, ca, cb):
    return lax.dot_general(
        a.astype(bf16), b.astype(bf16), (((ca,), (cb,)), ((), ())), preferred_element_type=f32
    )


def sigmoid(u):
    return 1.0 / (1.0 + jnp.exp(-u))


def norm_forward(x, gain):
    return x * lax.rsqrt(jnp.mean(x * x, axis=-1, keepdims=True) + norm_eps) * gain


def norm_backward(x, gain, grad):
    rate = lax.rsqrt(jnp.mean(x * x, axis=-1, keepdims=True) + norm_eps)
    unit = x * rate
    grad_gain = jnp.sum(grad * unit, axis=0, keepdims=True)
    scaled = grad * gain
    grad_x = rate * (scaled - unit * jnp.mean(scaled * unit, axis=-1, keepdims=True))
    return grad_x, grad_gain


def blocks_of(array, parity, size):
    block = array.shape[1] // size
    return jnp.concatenate(
        [array[:, i * block : (i + 1) * block] for i in range(parity, size, 2)], axis=1
    )


def keep_send(array, y, size):
    even, odd = blocks_of(array, 0, size), blocks_of(array, 1, size)
    lead = y == 0
    return jnp.where(lead, even, odd), jnp.where(lead, odd, even)


def put_halves(part, index_ref, part_ref, mine_ref, other_ref):
    rows = part.shape[0] // 2
    bit = index_ref[1]
    part_ref[...] = part
    mine_ref[...] = part_ref[pl.ds(pl.multiple_of(bit * rows, rows), rows), :]
    other_ref[...] = part_ref[pl.ds(pl.multiple_of((1 - bit) * rows, rows), rows), :]


def get_total(index_ref, near_ref, far_ref):
    lead = index_ref[1] == 0
    near, far = near_ref[...], far_ref[...]
    return jnp.concatenate([jnp.where(lead, near, far), jnp.where(lead, far, near)], axis=0)


def in_kernel(
    index_ref, stream_ref, gain_ref, w_ref, keep_ref, send_ref, proj_ref, *, level, size
):
    normed = norm_forward(stream_ref[...].astype(f32), gain_ref[level : level + 1, :])
    keep, send = keep_send(normed, index_ref[0], size)
    keep_ref[...] = keep.astype(bf16)
    send_ref[...] = send.astype(bf16).astype(f32)
    proj_ref[...] = mmb(normed, w_ref[...], 1, 0)


def in_sum_kernel(
    index_ref, mid_ref, near_ref, far_ref, gain_ref, w_ref,
    stream_ref, keep_ref, send_ref, proj_ref, *, level, size
):
    stream_ref[...] = mid_ref[...] + get_total(index_ref, near_ref, far_ref)
    in_kernel(
        index_ref, stream_ref, gain_ref, w_ref, keep_ref, send_ref, proj_ref,
        level=level, size=size,
    )


def conv_of(win_ref, taps, length):
    conv = taps[0:1] * win_ref[pl.ds(PAD, length), :]
    for tap in range(1, CONV):
        conv = conv + taps[tap : tap + 1] * win_ref[pl.ds(PAD - tap, length), :]
    return conv


def decay_of(col, row, length):
    rows = lax.broadcasted_iota(jnp.int32, (length, length), 0)
    cols = lax.broadcasted_iota(jnp.int32, (length, length), 1)
    keep = rows >= cols
    ratio = jnp.where(keep, jnp.exp(jnp.where(keep, col - row, 0.0)), 0.0)
    return rows, cols, ratio


def delta_kernel(
    y_ref, proj_ref, before_ref, taps_ref, col_ref, row_ref, beta_ref,
    ow_ref, uw_ref, solve_ref, mix_ref, send_ref, keep_ref, transfer_ref,
    win_ref, offset_ref,
):
    length = proj_ref.shape[0]
    for head in range(col_ref.shape[0]):
        base = head * WIDE
        win_ref[0:PAD, :] = before_ref[:, base : base + QKV]
        win_ref[pl.ds(PAD, length), :] = proj_ref[:, base : base + QKV]
        conv = conv_of(win_ref, taps_ref[:, head * QKV : (head + 1) * QKV].astype(f32), length)
        active = conv * sigmoid(conv)
        q_act = active[:, :DK]
        k_act = active[:, DK : 2 * DK]
        values = active[:, 2 * DK :]
        q = q_act * lax.rsqrt(jnp.sum(q_act * q_act, axis=-1, keepdims=True) + norm_eps)
        q = q * DK ** (-0.5)
        k = k_act * lax.rsqrt(jnp.sum(k_act * k_act, axis=-1, keepdims=True) + norm_eps)
        col = col_ref[head]
        row = row_ref[head]
        beta = beta_ref[head]
        rows, cols, ratio = decay_of(col, row, length)
        key_key = mm(k, k, 1, 1)
        query_key = mm(q, k, 1, 1)
        lower = jnp.where(rows > cols, beta * ratio * key_key, 0.0)
        solve = jnp.where(rows == cols, 1.0, 0.0)
        block = 1
        while block < length:
            here = (
                (rows // (2 * block) == cols // (2 * block))
                & (rows % (2 * block) >= block)
                & (cols % (2 * block) < block)
            )
            part = jnp.where(here, lower, 0.0)
            if block == 1:
                solve = solve - part
            else:
                solve = solve - mm(solve, mm(part, solve, 1, 0), 1, 0)
            block *= 2
        decay = jnp.exp(col)
        right = jnp.concatenate([beta * values, (beta * decay) * k], axis=1)
        uw = mm(solve, right, 1, 0)
        mix = ratio * query_key
        muw = mm(mix, uw, 1, 0)
        last = row[:, length - 1 :]
        ends = mm(uw, jnp.exp(last - col) * k, 0, 0)
        eye = jnp.where(
            lax.broadcasted_iota(jnp.int32, (DK, DK), 0)
            == lax.broadcasted_iota(jnp.int32, (DK, DK), 1),
            1.0,
            0.0,
        )
        transfer = jnp.exp(last) * eye - ends[DV:]
        offset_ref[...] = ends[:DV]
        ow_ref[head] = jnp.concatenate([muw[:, :DV], decay * q - muw[:, DV:]], axis=1)
        uw_ref[head] = uw
        solve_ref[head] = solve
        mix_ref[head] = mix
        transfer_ref[head] = transfer
        y = y_ref[0]
        send_ref[head, 0:DK, :] = transfer
        send_ref[head, DK : DK + HALF, :] = offset_ref[
            pl.ds(pl.multiple_of((1 - y) * HALF, HALF), HALF), :
        ]
        keep_ref[head] = offset_ref[pl.ds(pl.multiple_of(y * HALF, HALF), HALF), :]


def pair_kernel(
    y_ref, own_ref, keep_ref, other_ref, first_t_ref, second_t_ref, first_o_ref, pair_ref
):
    lead = y_ref[0] == 0
    for head in range(own_ref.shape[0]):
        own, other = own_ref[head], other_ref[head, 0:DK, :]
        keep, far = keep_ref[head], other_ref[head, DK : DK + HALF, :]
        first_t, second_t = jnp.where(lead, own, other), jnp.where(lead, other, own)
        first_o, second_o = jnp.where(lead, keep, far), jnp.where(lead, far, keep)
        first_t_ref[head] = first_t
        second_t_ref[head] = second_t
        first_o_ref[head] = first_o
        both = mm(jnp.concatenate([first_t, first_o], axis=0), second_t, 1, 0)
        pair_ref[head, 0:DK, :] = both[:DK]
        pair_ref[head, DK : DK + HALF, :] = both[DK:] + second_o


def window_kernel(near_ref, pair_ref, out_ref):
    for head in range(pair_ref.shape[0]):
        pair = pair_ref[head]
        out_ref[head] = mm(near_ref[head, DK : DK + HALF, :], pair[:DK], 1, 0) + pair[DK:]


def step_kernel(state_ref, pair_ref, out_ref):
    for head in range(state_ref.shape[0]):
        pair = pair_ref[head]
        out_ref[head] = mm(state_ref[head], pair[:DK], 1, 0) + pair[DK:]


def step_back_kernel(state_ref, pair_ref, offset_ref, out_ref):
    for head in range(state_ref.shape[0]):
        transfer = pair_ref[head, 0:DK, :]
        out_ref[head] = mm(state_ref[head], transfer, 1, 1) + offset_ref[head]


def last_kernel(
    y_ref, state_ref, near_ref, transfer_ref, offset_ref, mine_ref, other_ref, *, window
):
    lead = y_ref[0] == 0
    for head in range(state_ref.shape[0]):
        state = state_ref[head]
        if window:
            near = near_ref[head]
            state = mm(state, near[:DK], 1, 0) + near[DK:]
        moved = mm(state, transfer_ref[head], 1, 0) + offset_ref[head]
        mine_ref[head] = jnp.where(lead, state, moved)
        other_ref[head] = jnp.where(lead, moved, state)


def pair_back_kernel(y_ref, keep_ref, other_ref, first_t_ref, second_ref, pair_ref):
    lead = y_ref[0] == 0
    for head in range(keep_ref.shape[0]):
        keep, far = keep_ref[head], other_ref[head]
        first, second = jnp.where(lead, keep, far), jnp.where(lead, far, keep)
        second_ref[head] = second
        pair_ref[head] = first + mm(second, first_t_ref[head], 1, 1)


def last_back_kernel(y_ref, state_ref, transfer_ref, offset_ref, mine_ref, other_ref):
    lead = y_ref[0] == 0
    for head in range(state_ref.shape[0]):
        state = state_ref[head]
        moved = mm(state, transfer_ref[head], 1, 1) + offset_ref[head]
        mine_ref[head] = jnp.where(lead, moved, state)
        other_ref[head] = jnp.where(lead, state, moved)


def halves(y, mine, other):
    lead = y == 0
    return jnp.concatenate(
        [jnp.where(lead, mine, other), jnp.where(lead, other, mine)], axis=0
    )


def out_kernel(
    y_ref, mine_ref, other_ref, ow_ref, proj_ref, gain_ref, w_ref,
    state_ref, outputs_ref, gated_ref, near_ref, far_ref, part_ref, *, level,
):
    pieces = []
    for head in range(ow_ref.shape[0]):
        state = halves(y_ref[0], mine_ref[head], other_ref[head])
        state_ref[head] = state
        ow = ow_ref[head]
        outputs = ow[:, :DV] + mm(ow[:, DV:], state, 1, 1)
        outputs_ref[:, head * DV : (head + 1) * DV] = outputs
        z = proj_ref[:, head * WIDE + QKV : (head + 1) * WIDE]
        pieces.append((norm_forward(outputs, gain_ref[level : level + 1, :]) * (z * sigmoid(z))).astype(bf16))
    gated = jnp.concatenate(pieces, axis=1)
    gated_ref[...] = gated.astype(f32)
    put_halves(mmb(gated, w_ref[...], 1, 0), y_ref, part_ref, near_ref, far_ref)


def ffn_kernel(
    index_ref, stream_ref, near_ref, far_ref, gain_ref, wg_ref, wu_ref, wd_ref,
    mid_ref, keep_ref, send_ref, gate_ref, up_ref, mine_ref, other_ref, part_ref,
    *, level, size,
):
    mid = stream_ref[...].astype(f32) + get_total(index_ref, near_ref, far_ref)
    mid_ref[...] = mid
    normed = norm_forward(mid, gain_ref[level : level + 1, :])
    keep, send = keep_send(normed, index_ref[0], size)
    keep_ref[...] = keep.astype(bf16)
    half = mid.shape[1] // 2
    send_ref[:, :half] = send.astype(bf16).astype(f32)
    normed = normed.astype(bf16)
    gate = mmb(normed, wg_ref[...], 1, 0)
    up = mmb(normed, wu_ref[...], 1, 0)
    gate_ref[...] = gate
    up_ref[...] = up
    hidden = (gate * sigmoid(gate) * up).astype(bf16)
    send_ref[:, half:] = hidden.astype(f32)
    put_halves(mmb(hidden, wd_ref[...], 1, 0), index_ref, part_ref, mine_ref, other_ref)


def sum_kernel(index_ref, mid_ref, near_ref, far_ref, out_ref):
    out_ref[...] = (mid_ref[...] + get_total(index_ref, near_ref, far_ref)).astype(bf16)


def ffn_back_kernel(
    index_ref, grad_ref, gate_ref, up_ref, wg_ref, wu_ref, wd_ref,
    keep_ref, send_ref, mine_ref, other_ref, part_ref, *, size,
):
    back = grad_ref[...].astype(bf16)
    keep, send = keep_send(back.astype(f32), index_ref[0], size)
    keep_ref[...] = keep.astype(bf16)
    hidden = mmb(back, wd_ref[...], 1, 1)
    gate, up = gate_ref[...], up_ref[...]
    rate = sigmoid(gate)
    gu = (hidden * (gate * rate)).astype(bf16)
    gg = (hidden * up * (rate * (1.0 + gate * (1.0 - rate)))).astype(bf16)
    width = gate.shape[1]
    send_ref[:, : 2 * width] = jnp.concatenate([gg.astype(f32), gu.astype(f32)], axis=1)
    send_ref[:, 2 * width :] = send
    part = mmb(gg, wg_ref[...], 1, 1) + mmb(gu, wu_ref[...], 1, 1)
    put_halves(part, index_ref, part_ref, mine_ref, other_ref)


def out_back_kernel(
    y_ref, grad_ref, near_ref, far_ref, mid_ref, gain_ref, w_ref, outputs_ref, proj_ref,
    out_gain_ref, ow_ref,
    next_ref, back_keep_ref, back_send_ref, do_ref, dz_ref, dgain_ref, dout_gain_ref,
    send_ref, keep_ref,
    local_ref, *, level, size,
):
    grad_mid, grad_gain = norm_backward(
        mid_ref[...], gain_ref[level : level + 1, :], get_total(y_ref, near_ref, far_ref)
    )
    dgain_ref[...] = grad_gain
    grad = grad_ref[...].astype(f32) + grad_mid
    next_ref[...] = grad
    back = grad.astype(bf16)
    back_keep, back_send = keep_send(back.astype(f32), y_ref[0], size)
    back_keep_ref[...] = back_keep.astype(bf16)
    back_send_ref[...] = back_send
    gated = mmb(back, w_ref[...], 1, 1)
    gain = out_gain_ref[level : level + 1, :]
    total_gain = jnp.zeros_like(gain)
    y = y_ref[0]
    for head in range(ow_ref.shape[0]):
        span = slice(head * DV, (head + 1) * DV)
        outputs = outputs_ref[:, span]
        z = proj_ref[:, head * WIDE + QKV : (head + 1) * WIDE]
        rate = sigmoid(z)
        grad_h = gated[:, span]
        grad_n = grad_h * (z * rate)
        dz_ref[:, span] = (
            grad_h * norm_forward(outputs, gain) * (rate * (1.0 + z * (1.0 - rate)))
        )
        grad_o, gain_part = norm_backward(outputs, gain, grad_n)
        total_gain = total_gain + gain_part
        do_ref[:, span] = grad_o
        local_ref[...] = mm(grad_o, ow_ref[head][:, DV:], 0, 0)
        send_ref[head] = local_ref[pl.ds(pl.multiple_of((1 - y) * HALF, HALF), HALF), :]
        keep_ref[head] = local_ref[pl.ds(pl.multiple_of(y * HALF, HALF), HALF), :]
    dout_gain_ref[...] = total_gain


def delta_back_kernel(
    y_ref, mine_ref, other_ref, state_ref, uw_ref, solve_ref, mix_ref, do_ref,
    proj_ref, before_ref, taps_ref, col_ref, row_ref, beta_ref,
    dconv_ref, dtaps_ref, edge_ref,
    win_ref,
):
    length = proj_ref.shape[0]
    for head in range(col_ref.shape[0]):
        base = head * WIDE
        win_ref[0:PAD, :] = before_ref[:, base : base + QKV]
        win_ref[pl.ds(PAD, length), :] = proj_ref[:, base : base + QKV]
        taps = taps_ref[:, head * QKV : (head + 1) * QKV].astype(f32)
        conv = conv_of(win_ref, taps, length)
        rate = sigmoid(conv)
        active = conv * rate
        q_act = active[:, :DK]
        k_act = active[:, DK : 2 * DK]
        q_rate = lax.rsqrt(jnp.sum(q_act * q_act, axis=-1, keepdims=True) + norm_eps)
        k_rate = lax.rsqrt(jnp.sum(k_act * k_act, axis=-1, keepdims=True) + norm_eps)
        q_unit = q_act * q_rate
        k = k_act * k_rate
        q = q_unit * DK ** (-0.5)
        col = col_ref[head]
        row = row_ref[head]
        beta = beta_ref[head]
        rows, cols, ratio = decay_of(col, row, length)
        decay = jnp.exp(col)
        to_end = jnp.exp(row[:, length - 1 :] - col)
        state = state_ref[head]
        grad_end = halves(y_ref[0], mine_ref[head], other_ref[head])
        uw = uw_ref[head]
        grad_o = do_ref[:, head * DV : (head + 1) * DV]
        values_new = uw[:, :DV] - mmb(uw[:, DV:], state, 1, 1)
        grad_new = mmb(mix_ref[head], grad_o, 0, 0) + mmb(to_end * k, grad_end, 1, 1)
        grad_right = mmb(solve_ref[head], grad_new, 0, 0)
        grad_mix = jnp.where(rows >= cols, ratio * mmb(grad_o, values_new, 1, 1), 0.0)
        grad_low = jnp.where(
            rows > cols, -(beta * ratio) * mmb(grad_right, values_new, 1, 1), 0.0
        )
        grad_q = decay * mmb(grad_o, state, 1, 0) + mmb(grad_mix, k, 1, 0)
        grad_k = to_end * mmb(values_new, grad_end, 1, 0)
        grad_k = grad_k - (beta * decay) * mmb(grad_right, state, 1, 0)
        grad_k = grad_k + mmb(grad_low, k, 1, 0) + mmb(grad_low, k, 0, 0)
        grad_k = grad_k + mmb(grad_mix, q, 0, 0)
        grad_v = beta * grad_right
        grad_qa = (DK ** (-0.5)) * q_rate * (
            grad_q - q_unit * jnp.sum(grad_q * q_unit, axis=-1, keepdims=True)
        )
        grad_ka = k_rate * (grad_k - k * jnp.sum(grad_k * k, axis=-1, keepdims=True))
        grad_conv = jnp.concatenate([grad_qa, grad_ka, grad_v], axis=1) * (
            rate * (1.0 + conv * (1.0 - rate))
        )
        span = slice(head * QKV, (head + 1) * QKV)
        dconv_ref[:, span] = grad_conv
        edge_ref[:, span] = grad_conv[0:PAD]
        for tap in range(CONV):
            dtaps_ref[tap : tap + 1, span] = jnp.sum(
                grad_conv * win_ref[pl.ds(PAD - tap, length), :], axis=0, keepdims=True
            )


def in_back_kernel(
    index_ref, dconv_ref, after_ref, taps_ref, dz_ref, w_ref,
    gp_ref, mine_ref, other_ref, ext_ref, part_ref,
):
    length = dconv_ref.shape[0]
    ext_ref[pl.ds(0, length), :] = dconv_ref[...]
    ext_ref[pl.ds(length, PAD), :] = after_ref[...]
    taps = taps_ref[...].astype(f32)
    total = taps[0:1] * ext_ref[pl.ds(0, length), :]
    for tap in range(1, CONV):
        total = total + taps[tap : tap + 1] * ext_ref[pl.ds(tap, length), :]
    pieces = []
    for head in range(total.shape[1] // QKV):
        pieces.append(total[:, head * QKV : (head + 1) * QKV])
        pieces.append(dz_ref[:, head * DV : (head + 1) * DV])
    grad_proj = jnp.concatenate(pieces, axis=1).astype(bf16)
    gp_ref[...] = grad_proj.astype(f32)
    put_halves(mmb(grad_proj, w_ref[...], 1, 1), index_ref, part_ref, mine_ref, other_ref)


def norm_back_kernel(
    index_ref, grad_ref, near_ref, far_ref, stream_ref, gain_ref, out_ref, dgain_ref, *, level
):
    grad_x, grad_gain = norm_backward(
        stream_ref[...].astype(f32),
        gain_ref[level : level + 1, :],
        get_total(index_ref, near_ref, far_ref),
    )
    out_ref[...] = grad_ref[...] + grad_x
    dgain_ref[...] = grad_gain


def weight_block_kernel(
    n2_ref, own_ref, own_far_ref, ffn_ref, ffn_far_ref, back_ref, mid_ref, mid_far_ref,
    gated_ref, gated_far_ref, out_ref,
):
    half = back_ref.shape[1]
    width = own_ref.shape[1] - half
    both = 2 * width
    out_ref[:, :both] = mmb(n2_ref[...], ffn_ref[:, :both], 0, 0) + mmb(
        own_far_ref[:, :half], ffn_far_ref[:, :both], 0, 0
    )
    out_ref[:, both : both + width] = mmb(back_ref[...], own_ref[:, half:], 0, 0) + mmb(
        ffn_far_ref[:, both:], own_far_ref[:, half:], 0, 0
    )
    out_ref[:, both + width :] = mmb(mid_ref[...], gated_ref[...], 0, 0) + mmb(
        mid_far_ref[...], gated_far_ref[...], 0, 0
    )


def weight_in_kernel(a_ref, b_ref, a_far_ref, b_far_ref, out_ref):
    out_ref[...] = mmb(a_ref[...], b_ref[...], 0, 0) + mmb(a_far_ref[...], b_far_ref[...], 0, 0)


def shift(array, axis, by):
    length = lax.axis_size(axis)
    pairs = [(i, i + by) for i in range(length) if 0 <= i + by < length]
    return lax.ppermute(array, axis, pairs)


def swap(array, axis, bit):
    length = lax.axis_size(axis)
    return lax.ppermute(array, axis, [(i, i ^ bit) for i in range(length)])


def head_total(mine, other, name):
    with jax.named_scope("x_" + name):
        total = mine + swap(other, "head", 1)
        step = 2
        while step < lax.axis_size("head"):
            total = total + swap(total, "head", step)
            step *= 2
        return total, swap(total, "head", 1)


def after(array, mark):
    return lax.optimization_barrier((array, mark))[0]


def full_sum(array, axis):
    step = 1
    while step < lax.axis_size(axis):
        array = array + swap(array, axis, step)
        step *= 2
    return array


def outer_scatter(array):
    size = lax.axis_size("seq")
    groups = [[2 * o + p for o in range(size // 2)] for p in range(2)]
    return lax.psum_scatter(
        array, "seq", scatter_dimension=0, tiled=True, axis_index_groups=groups
    )


def prefix(local, transfer, y, level):
    send, keep = local
    heads = keep.shape[0]
    square = shape_of((heads, DK, DK))
    half = shape_of((heads, HALF, DK))
    outer = lax.axis_size("seq") // 2
    far = swap(send, "seq", 1)
    first_t, second_t, first_o, pair = call(
        pair_kernel,
        [square, square, half, shape_of((heads, DK + HALF, DK))],
        [y, transfer, keep, far],
        f"pair_{level}",
    )
    if outer == 4:
        near = shift(pair, "seq", 2)
        (moved,) = call(window_kernel, [half], [near, pair], f"window_{level}")
        state = shift(moved, "seq", 4)
    else:
        near = pair
        state = shift(pair[:, DK:], "seq", 2)
        for hop in range(outer - 2):
            (moved,) = call(step_kernel, [half], [state, pair], f"step_{level}_{hop}")
            state = shift(moved, "seq", 2)
    mine, other = call(
        functools.partial(last_kernel, window=outer == 4),
        [half, half],
        [y, state, near, first_t, first_o],
        f"last_{level}",
    )
    return mine, swap(other, "seq", 1), first_t, second_t, pair, near


def suffix(send, keep, kept, y, level):
    heads = keep.shape[0]
    half = shape_of((heads, HALF, DK))
    outer = lax.axis_size("seq") // 2
    far = swap(send, "seq", 1)
    second_o, pair_o = call(
        pair_back_kernel, [half, half], [y, keep, far, kept["first_t"]], f"pair_back_{level}"
    )
    state = shift(pair_o, "seq", -2)
    mark = state
    for hop in range(outer - 2):
        (moved,) = call(
            step_back_kernel, [half], [state, kept["pair"], pair_o], f"step_back_{level}_{hop}"
        )
        state = shift(moved, "seq", -2)
    mine, other = call(
        last_back_kernel,
        [half, half],
        [y, state, kept["second_t"], second_o],
        f"last_back_{level}",
    )
    return mine, swap(other, "seq", 1), mark


def layer_forward(start, shared, level, y):
    col, row, beta, gain_one, w_in, taps, out_gain, w_out, gain_two, w_gate, w_up, w_down = shared
    length, width = start[0].shape
    heads = col.shape[1]
    proj_width = w_in.shape[2]
    hidden_width = w_gate.shape[2]
    value_width = heads * DV
    size = lax.axis_size("seq")
    half_width = width // 2
    rows = shape_of((length // 2, width))
    whole = pltpu.VMEM((length, width), f32)
    kept_half = [shape_of((length, half_width), bf16), shape_of((length, half_width))]
    if len(start) == 1:
        stream = start[0]
        normed, normed_send, proj = call(
            functools.partial(in_kernel, level=level, size=size),
            kept_half + [shape_of((length, proj_width))],
            [y, stream, gain_one, (w_in, level)],
            f"in_{level}",
        )
    else:
        stream, normed, normed_send, proj = call(
            functools.partial(in_sum_kernel, level=level, size=size),
            [shape_of((length, width))] + kept_half + [shape_of((length, proj_width))],
            [y, *start, gain_one, (w_in, level)],
            f"in_{level}",
        )
    before = shift(proj[length - PAD :], "seq", 1)
    square = shape_of((heads, DK, DK))
    wide = shape_of((heads, length, DV + DK))
    inner = shape_of((heads, length, length))
    half = shape_of((heads, HALF, DK))
    ow, uw, solve, mix, send, keep, transfer = call(
        delta_kernel,
        [wide, wide, inner, inner, shape_of((heads, DK + HALF, DK)), half, square],
        [y, proj, before, (taps, level), (col, level), (row, level), (beta, level)],
        f"delta_{level}",
        [pltpu.VMEM((length + PAD, QKV), f32), pltpu.VMEM((DV, DK), f32)],
    )
    mine, other, first_t, second_t, pair, _ = prefix((send, keep), transfer, y, level)
    incoming, outputs, gated, near, far = call(
        functools.partial(out_kernel, level=level),
        [
            shape_of((heads, DV, DK)),
            shape_of((length, value_width)),
            shape_of((length, value_width)),
            rows,
            rows,
        ],
        [y, mine, other, ow, proj, out_gain, (w_out, level)],
        f"out_{level}",
        [whole],
    )
    total = head_total(near, far, f"out_{level}")
    mid, normed_two, ffn_send, gate, up, near, far = call(
        functools.partial(ffn_kernel, level=level, size=size),
        [
            shape_of((length, width)),
            shape_of((length, half_width), bf16),
            shape_of((length, half_width + hidden_width)),
            shape_of((length, hidden_width)),
            shape_of((length, hidden_width)),
            rows,
            rows,
        ],
        [y, stream, *total, gain_two, (w_gate, level), (w_up, level), (w_down, level)],
        f"ffn_{level}",
        [whole],
    )
    total = head_total(near, far, f"ffn_{level}")
    stored = dict(
        stream=stream, normed=normed, proj=proj, before=before, ow=ow, uw=uw, solve=solve,
        mix=mix, first_t=first_t, second_t=second_t, pair=pair, incoming=incoming,
        outputs=outputs, gated=gated, mid=mid, normed_two=normed_two, gate=gate, up=up,
        ffn_send=ffn_send, normed_far=swap(normed_send, "seq", 1),
        gated_far=swap(gated, "seq", 1), ffn_far=swap(ffn_send, "seq", 1),
    )
    return (mid, *total), stored


def layer_backward(grad, shared, level, kept, y, pending):
    col, row, beta, gain_one, w_in, taps, out_gain, w_out, gain_two, w_gate, w_up, w_down = shared
    length, width = grad.shape
    heads = col.shape[1]
    proj_width = w_in.shape[2]
    hidden_width = w_gate.shape[2]
    value_width = heads * DV
    qkv_width = heads * QKV
    size = lax.axis_size("seq")
    half_width = width // 2
    rows = shape_of((length // 2, width))
    whole = pltpu.VMEM((length, width), f32)
    back, back_send, near, far = call(
        functools.partial(ffn_back_kernel, size=size),
        [
            shape_of((length, half_width), bf16),
            shape_of((length, 2 * hidden_width + half_width)),
            rows,
            rows,
        ],
        [y, grad, kept["gate"], kept["up"], (w_gate, level), (w_up, level), (w_down, level)],
        f"ffn_back_{level}",
        [whole],
    )
    with jax.named_scope(f"x_ffn_far_{level}"):
        back_far = swap(back_send, "seq", 1)
    total = head_total(near, far, f"ffn_back_{level}")
    if pending is not None:
        pending = pending(near)
    half = shape_of((heads, HALF, DK))
    grad, mid_back, mid_send, grad_o, grad_z, dgain_two, dout_gain, send, keep = call(
        functools.partial(out_back_kernel, level=level, size=size),
        [
            shape_of((length, width)),
            shape_of((length, half_width), bf16),
            shape_of((length, half_width)),
            shape_of((length, value_width)),
            shape_of((length, value_width)),
            shape_of((1, width)),
            shape_of((1, DV)),
            half,
            half,
        ],
        [
            y, grad, *total, kept["mid"], gain_two, (w_out, level), kept["outputs"],
            kept["proj"], out_gain, kept["ow"],
        ],
        f"out_back_{level}",
        [pltpu.VMEM((DV, DK), f32)],
    )
    with jax.named_scope(f"x_mid_far_{level}"):
        mid_far = swap(mid_send, "seq", 1)
    mine, other, mark = suffix(send, keep, kept, y, level)
    (block_weights,) = call(
        weight_block_kernel,
        [shape_of((half_width, 3 * hidden_width + value_width))],
        [
            kept["normed_two"], kept["ffn_send"], kept["ffn_far"], back_send,
            after(back_far, mark), back, mid_back, mid_far, kept["gated"], kept["gated_far"],
        ],
        f"weights_block_{level}",
    )
    block_weights = outer_scatter(block_weights)
    dconv, dtaps, edge = call(
        delta_back_kernel,
        [
            shape_of((length, qkv_width)),
            shape_of((CONV, qkv_width)),
            shape_of((PAD, qkv_width)),
        ],
        [
            y, mine, other, kept["incoming"], kept["uw"], kept["solve"], kept["mix"], grad_o,
            kept["proj"], kept["before"], (taps, level), (col, level), (row, level),
            (beta, level),
        ],
        f"delta_back_{level}",
        [pltpu.VMEM((length + PAD, QKV), f32)],
    )
    grad_proj, near, far = call(
        in_back_kernel,
        [shape_of((length, proj_width)), rows, rows],
        [y, dconv, shift(edge, "seq", -1), (taps, level), grad_z, (w_in, level)],
        f"in_back_{level}",
        [pltpu.VMEM((length + PAD, qkv_width), f32), whole],
    )
    with jax.named_scope(f"x_in_far_{level}"):
        proj_far = swap(grad_proj, "seq", 1)

    def finish(mark):
        held = proj_far if mark is None else after(proj_far, mark)
        (in_weights,) = call(
            weight_in_kernel,
            [shape_of((half_width, proj_width))],
            [kept["normed"], grad_proj, kept["normed_far"], held],
            f"weights_in_{level}",
        )
        return outer_scatter(in_weights)

    total = head_total(near, far, f"in_back_{level}")
    grad, dgain_one = call(
        functools.partial(norm_back_kernel, level=level),
        [shape_of((length, width)), shape_of((1, width))],
        [y, grad, *total, kept["stream"], gain_one],
        f"norm_back_{level}",
    )
    return grad, (block_weights, dtaps, dgain_one, dout_gain, dgain_two), finish, pending


def body(
    tokens,
    cotangent,
    gate_code,
    beta_code,
    norm1_gain,
    weight_in,
    conv_weight,
    out_gain,
    weight_out,
    norm2_gain,
    weight_gate,
    weight_up,
    weight_down,
):
    y = jnp.stack([lax.axis_index("seq") % 2, lax.axis_index("head") % 2]).astype(jnp.int32)
    logdecay = -gate_code.astype(f32) * gate_unit
    beta_rate = jnp.transpose(beta_code.astype(f32) * beta_unit, (0, 2, 1))
    cumulated = jnp.transpose(jnp.cumsum(logdecay, axis=1), (0, 2, 1))
    shared = (
        cumulated[:, :, :, None],
        cumulated[:, :, None, :],
        beta_rate[:, :, :, None],
        norm1_gain,
        weight_in,
        conv_weight,
        out_gain,
        weight_out,
        norm2_gain,
        weight_gate,
        weight_up,
        weight_down,
    )
    start = (tokens,)
    kept = []
    for level in range(STACK_LEVELS):
        start, stored = layer_forward(start, shared, level, y)
        kept.append(stored)
    grad = cotangent
    parts = [None] * STACK_LEVELS
    in_weights = [None] * STACK_LEVELS
    finish = None
    for level in reversed(range(STACK_LEVELS)):
        grad, parts[level], finish, done = layer_backward(
            grad, shared, level, kept[level], y, finish
        )
        if done is not None:
            in_weights[level + 1] = done
    in_weights[0] = finish(None)
    (activations,) = call(sum_kernel, [shape_of(tokens.shape, bf16)], [y, *start], "finish")
    hidden_width = weight_gate.shape[2]
    block = [part[0] for part in parts]

    def join(pick):
        return jnp.stack([pick(piece) for piece in block])

    grad_gate = join(lambda piece: piece[:, :hidden_width])
    grad_up = join(lambda piece: piece[:, hidden_width : 2 * hidden_width])
    grad_down = join(lambda piece: piece[:, 2 * hidden_width : 3 * hidden_width].T)
    grad_out = join(lambda piece: piece[:, 3 * hidden_width :].T)
    grad_in = jnp.stack(in_weights)
    qkv_width = conv_weight.shape[2]
    width = tokens.shape[1]
    out_gain_part = full_sum(jnp.concatenate([part[3] for part in parts], axis=0), "head")
    small = jnp.concatenate(
        [part[1].reshape(1, -1) for part in parts]
        + [part[2] for part in parts]
        + [part[4] for part in parts]
        + [out_gain_part.reshape(1, -1)],
        axis=1,
    )
    small = full_sum(small, "seq")[0]
    sizes = [STACK_LEVELS * CONV * qkv_width, STACK_LEVELS * width, STACK_LEVELS * width]
    conv_grad = small[: sizes[0]].reshape(STACK_LEVELS, CONV, qkv_width)
    gain_one_grad = small[sizes[0] : sizes[0] + sizes[1]].reshape(STACK_LEVELS, width)
    gain_two_grad = small[sizes[0] + sizes[1] : sum(sizes)].reshape(STACK_LEVELS, width)
    out_gain_grad = small[sum(sizes) :].reshape(STACK_LEVELS, DV)
    return (
        activations,
        grad,
        gain_one_grad,
        grad_in,
        conv_grad,
        out_gain_grad,
        grad_out,
        gain_two_grad,
        grad_gate,
        grad_up,
        grad_down,
    )


def solution(mesh):
    in_specs = (
        P("seq", None),
        P("seq", None),
        P(None, "seq", "head"),
        P(None, "seq", "head"),
        P(),
        P(None, None, "head"),
        P(None, None, "head"),
        P(),
        P(None, "head", None),
        P(),
        P(None, None, "head"),
        P(None, None, "head"),
        P(None, "head", None),
    )
    out_specs = (
        P("seq", None),
        P("seq", None),
        P(),
        P(None, "seq", "head"),
        P(None, None, "head"),
        P(),
        P(None, "head", "seq"),
        P(),
        P(None, "seq", "head"),
        P(None, "seq", "head"),
        P(None, "head", "seq"),
    )
    return jax.shard_map(body, mesh=mesh, in_specs=in_specs, out_specs=out_specs, check_vma=False)
```

```python
import functools

import jax
import jax.numpy as jnp
from jax import lax
from jax.experimental import pallas as pl
from jax.experimental.pallas import tpu as pltpu
from jax.sharding import PartitionSpec as P


DK = 128
DV = 256
CONV = 4
STACK_LEVELS = 2
QKV = 2 * DK + DV
WIDE = 2 * DK + 2 * DV
HALF = DV // 2
PAD = 8

f32 = jnp.float32
bf16 = jnp.bfloat16
norm_eps = 1e-06
gate_unit = 1.0 / 1048576.0
beta_unit = 1.0 / 1024.0


def shape_of(dims, dtype=f32):
    return jax.ShapeDtypeStruct(tuple(dims), dtype)


def call(body, outs, args, scratch=()):
    specs, arrays = [], []
    for arg in args:
        if isinstance(arg, tuple):
            array, level = arg
            rest = (0,) * (array.ndim - 1)
            specs.append(
                pl.BlockSpec((None,) + array.shape[1:], functools.partial(at_level, level, rest))
            )
        elif arg.dtype == jnp.int32:
            array = arg
            specs.append(pl.BlockSpec(memory_space=pltpu.SMEM))
        else:
            array = arg
            specs.append(pl.BlockSpec(memory_space=pltpu.VMEM))
        arrays.append(array)
    return pl.pallas_call(
        body,
        grid=(1,),
        out_shape=tuple(outs),
        in_specs=specs,
        out_specs=tuple(pl.BlockSpec(memory_space=pltpu.VMEM) for _ in outs),
        scratch_shapes=list(scratch),
    )(*arrays)


def at_level(level, rest, _):
    return (level,) + rest


def mm(a, b, ca, cb):
    a_high, b_high = a.astype(bf16), b.astype(bf16)
    a_low = (a - a_high.astype(f32)).astype(bf16)
    b_low = (b - b_high.astype(f32)).astype(bf16)
    return mmb(a_high, b_high, ca, cb) + (mmb(a_high, b_low, ca, cb) + mmb(a_low, b_high, ca, cb))


def mmb(a, b, ca, cb):
    return lax.dot_general(
        a.astype(bf16), b.astype(bf16), (((ca,), (cb,)), ((), ())), preferred_element_type=f32
    )


def sigmoid(u):
    return 1.0 / (1.0 + jnp.exp(-u))


def norm_forward(x, gain):
    return x * lax.rsqrt(jnp.mean(x * x, axis=-1, keepdims=True) + norm_eps) * gain


def norm_backward(x, gain, grad):
    rate = lax.rsqrt(jnp.mean(x * x, axis=-1, keepdims=True) + norm_eps)
    unit = x * rate
    grad_gain = jnp.sum(grad * unit, axis=0, keepdims=True)
    scaled = grad * gain
    grad_x = rate * (scaled - unit * jnp.mean(scaled * unit, axis=-1, keepdims=True))
    return grad_x, grad_gain


def blocks_of(array, parity, size):
    block = array.shape[1] // size
    return jnp.concatenate(
        [array[:, i * block : (i + 1) * block] for i in range(parity, size, 2)], axis=1
    )


def keep_send(array, y, size):
    even, odd = blocks_of(array, 0, size), blocks_of(array, 1, size)
    lead = y == 0
    return jnp.where(lead, even, odd), jnp.where(lead, odd, even)


def put_halves(part, index_ref, part_ref, mine_ref, other_ref):
    rows = part.shape[0] // 2
    bit = index_ref[1]
    part_ref[...] = part
    mine_ref[...] = part_ref[pl.ds(pl.multiple_of(bit * rows, rows), rows), :]
    other_ref[...] = part_ref[pl.ds(pl.multiple_of((1 - bit) * rows, rows), rows), :]


def get_total(index_ref, near_ref, far_ref):
    lead = index_ref[1] == 0
    near, far = near_ref[...], far_ref[...]
    return jnp.concatenate([jnp.where(lead, near, far), jnp.where(lead, far, near)], axis=0)


def in_kernel(
    index_ref, stream_ref, gain_ref, w_ref, keep_ref, send_ref, proj_ref, *, level, size
):
    normed = norm_forward(stream_ref[...].astype(f32), gain_ref[level : level + 1, :])
    keep, send = keep_send(normed, index_ref[0], size)
    keep_ref[...] = keep.astype(bf16)
    send_ref[...] = send.astype(bf16).astype(f32)
    proj_ref[...] = mmb(normed, w_ref[...], 1, 0)


def in_sum_kernel(
    index_ref, mid_ref, near_ref, far_ref, gain_ref, w_ref,
    stream_ref, keep_ref, send_ref, proj_ref, *, level, size
):
    stream_ref[...] = mid_ref[...] + get_total(index_ref, near_ref, far_ref)
    in_kernel(
        index_ref, stream_ref, gain_ref, w_ref, keep_ref, send_ref, proj_ref,
        level=level, size=size,
    )


def conv_of(win_ref, taps, length):
    conv = taps[0:1] * win_ref[pl.ds(PAD, length), :]
    for tap in range(1, CONV):
        conv = conv + taps[tap : tap + 1] * win_ref[pl.ds(PAD - tap, length), :]
    return conv


def decay_of(col, row, length):
    rows = lax.broadcasted_iota(jnp.int32, (length, length), 0)
    cols = lax.broadcasted_iota(jnp.int32, (length, length), 1)
    keep = rows >= cols
    ratio = jnp.where(keep, jnp.exp(jnp.where(keep, col - row, 0.0)), 0.0)
    return rows, cols, ratio


def delta_kernel(
    y_ref, proj_ref, before_ref, taps_ref, col_ref, row_ref, beta_ref,
    ow_ref, uw_ref, solve_ref, mix_ref, send_ref, keep_ref, transfer_ref,
    win_ref, offset_ref,
):
    length = proj_ref.shape[0]
    for head in range(col_ref.shape[0]):
        base = head * WIDE
        win_ref[0:PAD, :] = before_ref[:, base : base + QKV]
        win_ref[pl.ds(PAD, length), :] = proj_ref[:, base : base + QKV]
        conv = conv_of(win_ref, taps_ref[:, head * QKV : (head + 1) * QKV].astype(f32), length)
        active = conv * sigmoid(conv)
        q_act = active[:, :DK]
        k_act = active[:, DK : 2 * DK]
        values = active[:, 2 * DK :]
        q = q_act * lax.rsqrt(jnp.sum(q_act * q_act, axis=-1, keepdims=True) + norm_eps)
        q = q * DK ** (-0.5)
        k = k_act * lax.rsqrt(jnp.sum(k_act * k_act, axis=-1, keepdims=True) + norm_eps)
        col = col_ref[head]
        row = row_ref[head]
        beta = beta_ref[head]
        rows, cols, ratio = decay_of(col, row, length)
        key_key = mm(k, k, 1, 1)
        query_key = mm(q, k, 1, 1)
        lower = jnp.where(rows > cols, beta * ratio * key_key, 0.0)
        solve = jnp.where(rows == cols, 1.0, 0.0)
        block = 1
        while block < length:
            here = (
                (rows // (2 * block) == cols // (2 * block))
                & (rows % (2 * block) >= block)
                & (cols % (2 * block) < block)
            )
            part = jnp.where(here, lower, 0.0)
            if block == 1:
                solve = solve - part
            else:
                solve = solve - mm(solve, mm(part, solve, 1, 0), 1, 0)
            block *= 2
        decay = jnp.exp(col)
        right = jnp.concatenate([beta * values, (beta * decay) * k], axis=1)
        uw = mm(solve, right, 1, 0)
        mix = ratio * query_key
        muw = mm(mix, uw, 1, 0)
        last = row[:, length - 1 :]
        ends = mm(uw, jnp.exp(last - col) * k, 0, 0)
        eye = jnp.where(
            lax.broadcasted_iota(jnp.int32, (DK, DK), 0)
            == lax.broadcasted_iota(jnp.int32, (DK, DK), 1),
            1.0,
            0.0,
        )
        transfer = jnp.exp(last) * eye - ends[DV:]
        offset_ref[...] = ends[:DV]
        ow_ref[head] = jnp.concatenate([muw[:, :DV], decay * q - muw[:, DV:]], axis=1)
        uw_ref[head] = uw
        solve_ref[head] = solve
        mix_ref[head] = mix
        transfer_ref[head] = transfer
        y = y_ref[0]
        send_ref[head, 0:DK, :] = transfer
        send_ref[head, DK : DK + HALF, :] = offset_ref[
            pl.ds(pl.multiple_of((1 - y) * HALF, HALF), HALF), :
        ]
        keep_ref[head] = offset_ref[pl.ds(pl.multiple_of(y * HALF, HALF), HALF), :]


def pair_kernel(
    y_ref, own_ref, keep_ref, other_ref, first_t_ref, second_t_ref, first_o_ref, pair_ref
):
    lead = y_ref[0] == 0
    for head in range(own_ref.shape[0]):
        own, other = own_ref[head], other_ref[head, 0:DK, :]
        keep, far = keep_ref[head], other_ref[head, DK : DK + HALF, :]
        first_t, second_t = jnp.where(lead, own, other), jnp.where(lead, other, own)
        first_o, second_o = jnp.where(lead, keep, far), jnp.where(lead, far, keep)
        first_t_ref[head] = first_t
        second_t_ref[head] = second_t
        first_o_ref[head] = first_o
        both = mm(jnp.concatenate([first_t, first_o], axis=0), second_t, 1, 0)
        pair_ref[head, 0:DK, :] = both[:DK]
        pair_ref[head, DK : DK + HALF, :] = both[DK:] + second_o


def window_kernel(near_ref, pair_ref, out_ref):
    for head in range(pair_ref.shape[0]):
        pair = pair_ref[head]
        out_ref[head] = mm(near_ref[head, DK : DK + HALF, :], pair[:DK], 1, 0) + pair[DK:]


def step_kernel(state_ref, pair_ref, out_ref):
    for head in range(state_ref.shape[0]):
        pair = pair_ref[head]
        out_ref[head] = mm(state_ref[head], pair[:DK], 1, 0) + pair[DK:]


def step_back_kernel(state_ref, pair_ref, offset_ref, out_ref):
    for head in range(state_ref.shape[0]):
        transfer = pair_ref[head, 0:DK, :]
        out_ref[head] = mm(state_ref[head], transfer, 1, 1) + offset_ref[head]


def last_kernel(
    y_ref, state_ref, near_ref, transfer_ref, offset_ref, mine_ref, other_ref, *, window
):
    lead = y_ref[0] == 0
    for head in range(state_ref.shape[0]):
        state = state_ref[head]
        if window:
            near = near_ref[head]
            state = mm(state, near[:DK], 1, 0) + near[DK:]
        moved = mm(state, transfer_ref[head], 1, 0) + offset_ref[head]
        mine_ref[head] = jnp.where(lead, state, moved)
        other_ref[head] = jnp.where(lead, moved, state)


def pair_back_kernel(y_ref, keep_ref, other_ref, first_t_ref, second_ref, pair_ref):
    lead = y_ref[0] == 0
    for head in range(keep_ref.shape[0]):
        keep, far = keep_ref[head], other_ref[head]
        first, second = jnp.where(lead, keep, far), jnp.where(lead, far, keep)
        second_ref[head] = second
        pair_ref[head] = first + mm(second, first_t_ref[head], 1, 1)


def last_back_kernel(y_ref, state_ref, transfer_ref, offset_ref, mine_ref, other_ref):
    lead = y_ref[0] == 0
    for head in range(state_ref.shape[0]):
        state = state_ref[head]
        moved = mm(state, transfer_ref[head], 1, 1) + offset_ref[head]
        mine_ref[head] = jnp.where(lead, moved, state)
        other_ref[head] = jnp.where(lead, state, moved)


def halves(y, mine, other):
    lead = y == 0
    return jnp.concatenate(
        [jnp.where(lead, mine, other), jnp.where(lead, other, mine)], axis=0
    )


def out_kernel(
    y_ref, mine_ref, other_ref, ow_ref, proj_ref, gain_ref, w_ref,
    state_ref, outputs_ref, gated_ref, near_ref, far_ref, part_ref, *, level,
):
    pieces = []
    for head in range(ow_ref.shape[0]):
        state = halves(y_ref[0], mine_ref[head], other_ref[head])
        state_ref[head] = state
        ow = ow_ref[head]
        outputs = ow[:, :DV] + mm(ow[:, DV:], state, 1, 1)
        outputs_ref[:, head * DV : (head + 1) * DV] = outputs
        z = proj_ref[:, head * WIDE + QKV : (head + 1) * WIDE]
        pieces.append((norm_forward(outputs, gain_ref[level : level + 1, :]) * (z * sigmoid(z))).astype(bf16))
    gated = jnp.concatenate(pieces, axis=1)
    gated_ref[...] = gated.astype(f32)
    put_halves(mmb(gated, w_ref[...], 1, 0), y_ref, part_ref, near_ref, far_ref)


def ffn_kernel(
    index_ref, stream_ref, near_ref, far_ref, gain_ref, wg_ref, wu_ref, wd_ref,
    mid_ref, keep_ref, send_ref, gate_ref, up_ref, mine_ref, other_ref, part_ref,
    *, level, size,
):
    mid = stream_ref[...].astype(f32) + get_total(index_ref, near_ref, far_ref)
    mid_ref[...] = mid
    normed = norm_forward(mid, gain_ref[level : level + 1, :])
    keep, send = keep_send(normed, index_ref[0], size)
    keep_ref[...] = keep.astype(bf16)
    half = mid.shape[1] // 2
    send_ref[:, :half] = send.astype(bf16).astype(f32)
    normed = normed.astype(bf16)
    gate = mmb(normed, wg_ref[...], 1, 0)
    up = mmb(normed, wu_ref[...], 1, 0)
    gate_ref[...] = gate
    up_ref[...] = up
    hidden = (gate * sigmoid(gate) * up).astype(bf16)
    send_ref[:, half:] = hidden.astype(f32)
    put_halves(mmb(hidden, wd_ref[...], 1, 0), index_ref, part_ref, mine_ref, other_ref)


def sum_kernel(index_ref, mid_ref, near_ref, far_ref, out_ref):
    out_ref[...] = (mid_ref[...] + get_total(index_ref, near_ref, far_ref)).astype(bf16)


def ffn_back_kernel(
    index_ref, grad_ref, gate_ref, up_ref, wg_ref, wu_ref, wd_ref,
    keep_ref, send_ref, mine_ref, other_ref, part_ref, *, size,
):
    back = grad_ref[...].astype(bf16)
    keep, send = keep_send(back.astype(f32), index_ref[0], size)
    keep_ref[...] = keep.astype(bf16)
    hidden = mmb(back, wd_ref[...], 1, 1)
    gate, up = gate_ref[...], up_ref[...]
    rate = sigmoid(gate)
    gu = (hidden * (gate * rate)).astype(bf16)
    gg = (hidden * up * (rate * (1.0 + gate * (1.0 - rate)))).astype(bf16)
    width = gate.shape[1]
    send_ref[:, : 2 * width] = jnp.concatenate([gg.astype(f32), gu.astype(f32)], axis=1)
    send_ref[:, 2 * width :] = send
    part = mmb(gg, wg_ref[...], 1, 1) + mmb(gu, wu_ref[...], 1, 1)
    put_halves(part, index_ref, part_ref, mine_ref, other_ref)


def out_back_kernel(
    y_ref, grad_ref, near_ref, far_ref, mid_ref, gain_ref, w_ref, outputs_ref, proj_ref,
    out_gain_ref, ow_ref,
    next_ref, back_keep_ref, back_send_ref, do_ref, dz_ref, dgain_ref, dout_gain_ref,
    send_ref, keep_ref,
    local_ref, *, level, size,
):
    grad_mid, grad_gain = norm_backward(
        mid_ref[...], gain_ref[level : level + 1, :], get_total(y_ref, near_ref, far_ref)
    )
    dgain_ref[...] = grad_gain
    grad = grad_ref[...].astype(f32) + grad_mid
    next_ref[...] = grad
    back = grad.astype(bf16)
    back_keep, back_send = keep_send(back.astype(f32), y_ref[0], size)
    back_keep_ref[...] = back_keep.astype(bf16)
    back_send_ref[...] = back_send
    gated = mmb(back, w_ref[...], 1, 1)
    gain = out_gain_ref[level : level + 1, :]
    total_gain = jnp.zeros_like(gain)
    y = y_ref[0]
    for head in range(ow_ref.shape[0]):
        span = slice(head * DV, (head + 1) * DV)
        outputs = outputs_ref[:, span]
        z = proj_ref[:, head * WIDE + QKV : (head + 1) * WIDE]
        rate = sigmoid(z)
        grad_h = gated[:, span]
        grad_n = grad_h * (z * rate)
        dz_ref[:, span] = (
            grad_h * norm_forward(outputs, gain) * (rate * (1.0 + z * (1.0 - rate)))
        )
        grad_o, gain_part = norm_backward(outputs, gain, grad_n)
        total_gain = total_gain + gain_part
        do_ref[:, span] = grad_o
        local_ref[...] = mm(grad_o, ow_ref[head][:, DV:], 0, 0)
        send_ref[head] = local_ref[pl.ds(pl.multiple_of((1 - y) * HALF, HALF), HALF), :]
        keep_ref[head] = local_ref[pl.ds(pl.multiple_of(y * HALF, HALF), HALF), :]
    dout_gain_ref[...] = total_gain


def delta_back_kernel(
    y_ref, mine_ref, other_ref, state_ref, uw_ref, solve_ref, mix_ref, do_ref,
    proj_ref, before_ref, taps_ref, col_ref, row_ref, beta_ref,
    dconv_ref, dtaps_ref, edge_ref,
    win_ref,
):
    length = proj_ref.shape[0]
    for head in range(col_ref.shape[0]):
        base = head * WIDE
        win_ref[0:PAD, :] = before_ref[:, base : base + QKV]
        win_ref[pl.ds(PAD, length), :] = proj_ref[:, base : base + QKV]
        taps = taps_ref[:, head * QKV : (head + 1) * QKV].astype(f32)
        conv = conv_of(win_ref, taps, length)
        rate = sigmoid(conv)
        active = conv * rate
        q_act = active[:, :DK]
        k_act = active[:, DK : 2 * DK]
        q_rate = lax.rsqrt(jnp.sum(q_act * q_act, axis=-1, keepdims=True) + norm_eps)
        k_rate = lax.rsqrt(jnp.sum(k_act * k_act, axis=-1, keepdims=True) + norm_eps)
        q_unit = q_act * q_rate
        k = k_act * k_rate
        q = q_unit * DK ** (-0.5)
        col = col_ref[head]
        row = row_ref[head]
        beta = beta_ref[head]
        rows, cols, ratio = decay_of(col, row, length)
        decay = jnp.exp(col)
        to_end = jnp.exp(row[:, length - 1 :] - col)
        state = state_ref[head]
        grad_end = halves(y_ref[0], mine_ref[head], other_ref[head])
        uw = uw_ref[head]
        grad_o = do_ref[:, head * DV : (head + 1) * DV]
        values_new = uw[:, :DV] - mmb(uw[:, DV:], state, 1, 1)
        grad_new = mmb(mix_ref[head], grad_o, 0, 0) + mmb(to_end * k, grad_end, 1, 1)
        grad_right = mmb(solve_ref[head], grad_new, 0, 0)
        grad_mix = jnp.where(rows >= cols, ratio * mmb(grad_o, values_new, 1, 1), 0.0)
        grad_low = jnp.where(
            rows > cols, -(beta * ratio) * mmb(grad_right, values_new, 1, 1), 0.0
        )
        grad_q = decay * mmb(grad_o, state, 1, 0) + mmb(grad_mix, k, 1, 0)
        grad_k = to_end * mmb(values_new, grad_end, 1, 0)
        grad_k = grad_k - (beta * decay) * mmb(grad_right, state, 1, 0)
        grad_k = grad_k + mmb(grad_low, k, 1, 0) + mmb(grad_low, k, 0, 0)
        grad_k = grad_k + mmb(grad_mix, q, 0, 0)
        grad_v = beta * grad_right
        grad_qa = (DK ** (-0.5)) * q_rate * (
            grad_q - q_unit * jnp.sum(grad_q * q_unit, axis=-1, keepdims=True)
        )
        grad_ka = k_rate * (grad_k - k * jnp.sum(grad_k * k, axis=-1, keepdims=True))
        grad_conv = jnp.concatenate([grad_qa, grad_ka, grad_v], axis=1) * (
            rate * (1.0 + conv * (1.0 - rate))
        )
        span = slice(head * QKV, (head + 1) * QKV)
        dconv_ref[:, span] = grad_conv
        edge_ref[:, span] = grad_conv[0:PAD]
        for tap in range(CONV):
            dtaps_ref[tap : tap + 1, span] = jnp.sum(
                grad_conv * win_ref[pl.ds(PAD - tap, length), :], axis=0, keepdims=True
            )


def in_back_kernel(
    index_ref, dconv_ref, after_ref, taps_ref, dz_ref, w_ref,
    gp_ref, mine_ref, other_ref, ext_ref, part_ref,
):
    length = dconv_ref.shape[0]
    ext_ref[pl.ds(0, length), :] = dconv_ref[...]
    ext_ref[pl.ds(length, PAD), :] = after_ref[...]
    taps = taps_ref[...].astype(f32)
    total = taps[0:1] * ext_ref[pl.ds(0, length), :]
    for tap in range(1, CONV):
        total = total + taps[tap : tap + 1] * ext_ref[pl.ds(tap, length), :]
    pieces = []
    for head in range(total.shape[1] // QKV):
        pieces.append(total[:, head * QKV : (head + 1) * QKV])
        pieces.append(dz_ref[:, head * DV : (head + 1) * DV])
    grad_proj = jnp.concatenate(pieces, axis=1).astype(bf16)
    gp_ref[...] = grad_proj.astype(f32)
    put_halves(mmb(grad_proj, w_ref[...], 1, 1), index_ref, part_ref, mine_ref, other_ref)


def norm_back_kernel(
    index_ref, grad_ref, near_ref, far_ref, stream_ref, gain_ref, out_ref, dgain_ref, *, level
):
    grad_x, grad_gain = norm_backward(
        stream_ref[...].astype(f32),
        gain_ref[level : level + 1, :],
        get_total(index_ref, near_ref, far_ref),
    )
    out_ref[...] = grad_ref[...] + grad_x
    dgain_ref[...] = grad_gain


def weight_block_kernel(
    n2_ref, own_ref, own_far_ref, ffn_ref, ffn_far_ref, back_ref, mid_ref, mid_far_ref,
    gated_ref, gated_far_ref, out_ref,
):
    half = back_ref.shape[1]
    width = own_ref.shape[1] - half
    both = 2 * width
    out_ref[:, :both] = mmb(n2_ref[...], ffn_ref[:, :both], 0, 0) + mmb(
        own_far_ref[:, :half], ffn_far_ref[:, :both], 0, 0
    )
    out_ref[:, both : both + width] = mmb(back_ref[...], own_ref[:, half:], 0, 0) + mmb(
        ffn_far_ref[:, both:], own_far_ref[:, half:], 0, 0
    )
    out_ref[:, both + width :] = mmb(mid_ref[...], gated_ref[...], 0, 0) + mmb(
        mid_far_ref[...], gated_far_ref[...], 0, 0
    )


def weight_in_kernel(a_ref, b_ref, a_far_ref, b_far_ref, out_ref):
    out_ref[...] = mmb(a_ref[...], b_ref[...], 0, 0) + mmb(a_far_ref[...], b_far_ref[...], 0, 0)


def shift(array, axis, by):
    length = lax.axis_size(axis)
    pairs = [(i, i + by) for i in range(length) if 0 <= i + by < length]
    return lax.ppermute(array, axis, pairs)


def swap(array, axis, bit):
    length = lax.axis_size(axis)
    return lax.ppermute(array, axis, [(i, i ^ bit) for i in range(length)])


def head_total(mine, other):
    total = mine + swap(other, "head", 1)
    step = 2
    while step < lax.axis_size("head"):
        total = total + swap(total, "head", step)
        step *= 2
    return total, swap(total, "head", 1)


def far_swap(array):
    return swap(array, "seq", 1)


def after(array, mark):
    return lax.optimization_barrier((array, mark))[0]


def full_sum(array, axis):
    step = 1
    while step < lax.axis_size(axis):
        array = array + swap(array, axis, step)
        step *= 2
    return array


def outer_scatter(array):
    size = lax.axis_size("seq")
    groups = [[2 * o + p for o in range(size // 2)] for p in range(2)]
    return lax.psum_scatter(array, "seq", scatter_dimension=0, tiled=True, axis_index_groups=groups)


def prefix(local, transfer, y):
    send, keep = local
    heads = keep.shape[0]
    square = shape_of((heads, DK, DK))
    half = shape_of((heads, HALF, DK))
    outer = lax.axis_size("seq") // 2
    far = swap(send, "seq", 1)
    first_t, second_t, first_o, pair = call(
        pair_kernel,
        [square, square, half, shape_of((heads, DK + HALF, DK))],
        [y, transfer, keep, far],
    )
    if outer == 4:
        near = shift(pair, "seq", 2)
        (moved,) = call(window_kernel, [half], [near, pair])
        state = shift(moved, "seq", 4)
    else:
        near = pair
        state = shift(pair[:, DK:], "seq", 2)
        for _ in range(outer - 2):
            (moved,) = call(step_kernel, [half], [state, pair])
            state = shift(moved, "seq", 2)
    mine, other = call(
        functools.partial(last_kernel, window=outer == 4),
        [half, half],
        [y, state, near, first_t, first_o],
    )
    return mine, swap(other, "seq", 1), first_t, second_t, pair, near


def suffix(send, keep, kept, y):
    heads = keep.shape[0]
    half = shape_of((heads, HALF, DK))
    outer = lax.axis_size("seq") // 2
    far = swap(send, "seq", 1)
    second_o, pair_o = call(pair_back_kernel, [half, half], [y, keep, far, kept["first_t"]])
    state = shift(pair_o, "seq", -2)
    mark = state
    for hop in range(outer - 2):
        (moved,) = call(step_back_kernel, [half], [state, kept["pair"], pair_o])
        if hop == 0:
            mark = moved
        state = shift(moved, "seq", -2)
    mine, other = call(last_back_kernel, [half, half], [y, state, kept["second_t"], second_o])
    return mine, swap(other, "seq", 1), mark


def layer_forward(start, shared, level, y):
    col, row, beta, gain_one, w_in, taps, out_gain, w_out, gain_two, w_gate, w_up, w_down = shared
    length, width = start[0].shape
    heads = col.shape[1]
    proj_width = w_in.shape[2]
    hidden_width = w_gate.shape[2]
    value_width = heads * DV
    size = lax.axis_size("seq")
    half_width = width // 2
    rows = shape_of((length // 2, width))
    whole = pltpu.VMEM((length, width), f32)
    kept_half = [shape_of((length, half_width), bf16), shape_of((length, half_width))]
    if len(start) == 1:
        stream = start[0]
        normed, normed_send, proj = call(
            functools.partial(in_kernel, level=level, size=size),
            kept_half + [shape_of((length, proj_width))],
            [y, stream, gain_one, (w_in, level)],
        )
    else:
        stream, normed, normed_send, proj = call(
            functools.partial(in_sum_kernel, level=level, size=size),
            [shape_of((length, width))] + kept_half + [shape_of((length, proj_width))],
            [y, *start, gain_one, (w_in, level)],
        )
    before = shift(proj[length - PAD :], "seq", 1)
    square = shape_of((heads, DK, DK))
    wide = shape_of((heads, length, DV + DK))
    inner = shape_of((heads, length, length))
    half = shape_of((heads, HALF, DK))
    ow, uw, solve, mix, send, keep, transfer = call(
        delta_kernel,
        [wide, wide, inner, inner, shape_of((heads, DK + HALF, DK)), half, square],
        [y, proj, before, (taps, level), (col, level), (row, level), (beta, level)],
        [pltpu.VMEM((length + PAD, QKV), f32), pltpu.VMEM((DV, DK), f32)],
    )
    mine, other, first_t, second_t, pair, _ = prefix((send, keep), transfer, y)
    incoming, outputs, gated, near, far = call(
        functools.partial(out_kernel, level=level),
        [
            shape_of((heads, DV, DK)),
            shape_of((length, value_width)),
            shape_of((length, value_width)),
            rows,
            rows,
        ],
        [y, mine, other, ow, proj, out_gain, (w_out, level)],
        [whole],
    )
    total = head_total(near, far)
    mid, normed_two, ffn_send, gate, up, near, far = call(
        functools.partial(ffn_kernel, level=level, size=size),
        [
            shape_of((length, width)),
            shape_of((length, half_width), bf16),
            shape_of((length, half_width + hidden_width)),
            shape_of((length, hidden_width)),
            shape_of((length, hidden_width)),
            rows,
            rows,
        ],
        [y, stream, *total, gain_two, (w_gate, level), (w_up, level), (w_down, level)],
        [whole],
    )
    total = head_total(near, far)
    stored = dict(
        stream=stream, normed=normed, proj=proj, before=before, ow=ow, uw=uw, solve=solve,
        mix=mix, first_t=first_t, second_t=second_t, pair=pair, incoming=incoming,
        outputs=outputs, gated=gated, mid=mid, normed_two=normed_two, gate=gate, up=up,
        ffn_send=ffn_send, normed_far=far_swap(after(normed_send, gated)),
        gated_far=far_swap(gated), ffn_far=far_swap(ffn_send),
    )
    return (mid, *total), stored


def layer_backward(grad, shared, level, kept, y, pending):
    col, row, beta, gain_one, w_in, taps, out_gain, w_out, gain_two, w_gate, w_up, w_down = shared
    length, width = grad.shape
    heads = col.shape[1]
    proj_width = w_in.shape[2]
    hidden_width = w_gate.shape[2]
    value_width = heads * DV
    qkv_width = heads * QKV
    size = lax.axis_size("seq")
    half_width = width // 2
    rows = shape_of((length // 2, width))
    whole = pltpu.VMEM((length, width), f32)
    back, back_send, near, far = call(
        functools.partial(ffn_back_kernel, size=size),
        [
            shape_of((length, half_width), bf16),
            shape_of((length, 2 * hidden_width + half_width)),
            rows,
            rows,
        ],
        [y, grad, kept["gate"], kept["up"], (w_gate, level), (w_up, level), (w_down, level)],
        [whole],
    )
    back_far = far_swap(back_send)
    total = head_total(near, far)
    if pending is not None:
        pending = pending(near)
    half = shape_of((heads, HALF, DK))
    grad, mid_back, mid_send, grad_o, grad_z, dgain_two, dout_gain, send, keep = call(
        functools.partial(out_back_kernel, level=level, size=size),
        [
            shape_of((length, width)),
            shape_of((length, half_width), bf16),
            shape_of((length, half_width)),
            shape_of((length, value_width)),
            shape_of((length, value_width)),
            shape_of((1, width)),
            shape_of((1, DV)),
            half,
            half,
        ],
        [
            y, grad, *total, kept["mid"], gain_two, (w_out, level), kept["outputs"],
            kept["proj"], out_gain, kept["ow"],
        ],
        [pltpu.VMEM((DV, DK), f32)],
    )
    mid_far = far_swap(mid_send)
    mine, other, mark = suffix(send, keep, kept, y)
    (block_weights,) = call(
        weight_block_kernel,
        [shape_of((half_width, 3 * hidden_width + value_width))],
        [
            kept["normed_two"], kept["ffn_send"], kept["ffn_far"], back_send,
            after(back_far, mark), back, mid_back, mid_far, kept["gated"], kept["gated_far"],
        ],
    )
    block_weights = outer_scatter(block_weights)
    dconv, dtaps, edge = call(
        delta_back_kernel,
        [
            shape_of((length, qkv_width)),
            shape_of((CONV, qkv_width)),
            shape_of((PAD, qkv_width)),
        ],
        [
            y, mine, other, kept["incoming"], kept["uw"], kept["solve"], kept["mix"], grad_o,
            kept["proj"], kept["before"], (taps, level), (col, level), (row, level),
            (beta, level),
        ],
        [pltpu.VMEM((length + PAD, QKV), f32)],
    )
    grad_proj, near, far = call(
        in_back_kernel,
        [shape_of((length, proj_width)), rows, rows],
        [y, dconv, shift(edge, "seq", -1), (taps, level), grad_z, (w_in, level)],
        [pltpu.VMEM((length + PAD, qkv_width), f32), whole],
    )
    proj_far = far_swap(grad_proj)

    def finish(mark):
        held = proj_far if mark is None else after(proj_far, mark)
        (in_weights,) = call(
            weight_in_kernel,
            [shape_of((half_width, proj_width))],
            [kept["normed"], grad_proj, kept["normed_far"], held],
        )
        return outer_scatter(in_weights)

    total = head_total(near, far)
    grad, dgain_one = call(
        functools.partial(norm_back_kernel, level=level),
        [shape_of((length, width)), shape_of((1, width))],
        [y, grad, *total, kept["stream"], gain_one],
    )
    return grad, (block_weights, dtaps, dgain_one, dout_gain, dgain_two), finish, pending


def body(
    tokens,
    cotangent,
    gate_code,
    beta_code,
    norm1_gain,
    weight_in,
    conv_weight,
    out_gain,
    weight_out,
    norm2_gain,
    weight_gate,
    weight_up,
    weight_down,
):
    y = jnp.stack([lax.axis_index("seq") % 2, lax.axis_index("head") % 2]).astype(jnp.int32)
    logdecay = -gate_code.astype(f32) * gate_unit
    beta_rate = jnp.transpose(beta_code.astype(f32) * beta_unit, (0, 2, 1))
    cumulated = jnp.transpose(jnp.cumsum(logdecay, axis=1), (0, 2, 1))
    shared = (
        cumulated[:, :, :, None],
        cumulated[:, :, None, :],
        beta_rate[:, :, :, None],
        norm1_gain,
        weight_in,
        conv_weight,
        out_gain,
        weight_out,
        norm2_gain,
        weight_gate,
        weight_up,
        weight_down,
    )
    start = (tokens,)
    kept = []
    for level in range(STACK_LEVELS):
        start, stored = layer_forward(start, shared, level, y)
        kept.append(stored)
    grad = cotangent
    parts = [None] * STACK_LEVELS
    in_weights = [None] * STACK_LEVELS
    finish = None
    for level in reversed(range(STACK_LEVELS)):
        grad, parts[level], finish, done = layer_backward(
            grad, shared, level, kept[level], y, finish
        )
        if done is not None:
            in_weights[level + 1] = done
    in_weights[0] = finish(None)
    (activations,) = call(sum_kernel, [shape_of(tokens.shape, bf16)], [y, *start])
    hidden_width = weight_gate.shape[2]
    block = [part[0] for part in parts]

    def join(pick):
        return jnp.stack([pick(piece) for piece in block])

    grad_gate = join(lambda piece: piece[:, :hidden_width])
    grad_up = join(lambda piece: piece[:, hidden_width : 2 * hidden_width])
    grad_down = join(lambda piece: piece[:, 2 * hidden_width : 3 * hidden_width].T)
    grad_out = join(lambda piece: piece[:, 3 * hidden_width :].T)
    grad_in = jnp.stack(in_weights)
    qkv_width = conv_weight.shape[2]
    width = tokens.shape[1]
    out_gain_part = full_sum(jnp.concatenate([part[3] for part in parts], axis=0), "head")
    small = jnp.concatenate(
        [part[1].reshape(1, -1) for part in parts]
        + [part[2] for part in parts]
        + [part[4] for part in parts]
        + [out_gain_part.reshape(1, -1)],
        axis=1,
    )
    small = full_sum(small, "seq")[0]
    sizes = [STACK_LEVELS * CONV * qkv_width, STACK_LEVELS * width, STACK_LEVELS * width]
    conv_grad = small[: sizes[0]].reshape(STACK_LEVELS, CONV, qkv_width)
    gain_one_grad = small[sizes[0] : sizes[0] + sizes[1]].reshape(STACK_LEVELS, width)
    gain_two_grad = small[sizes[0] + sizes[1] : sum(sizes)].reshape(STACK_LEVELS, width)
    out_gain_grad = small[sum(sizes) :].reshape(STACK_LEVELS, DV)
    return (
        activations,
        grad,
        gain_one_grad,
        grad_in,
        conv_grad,
        out_gain_grad,
        grad_out,
        gain_two_grad,
        grad_gate,
        grad_up,
        grad_down,
    )


def solution(mesh):
    in_specs = (
        P("seq", None),
        P("seq", None),
        P(None, "seq", "head"),
        P(None, "seq", "head"),
        P(),
        P(None, None, "head"),
        P(None, None, "head"),
        P(),
        P(None, "head", None),
        P(),
        P(None, None, "head"),
        P(None, None, "head"),
        P(None, "head", None),
    )
    out_specs = (
        P("seq", None),
        P("seq", None),
        P(),
        P(None, "seq", "head"),
        P(None, None, "head"),
        P(),
        P(None, "head", "seq"),
        P(),
        P(None, "seq", "head"),
        P(None, "seq", "head"),
        P(None, "head", "seq"),
    )

    return jax.shard_map(body, mesh=mesh, in_specs=in_specs, out_specs=out_specs, check_vma=False)
```

```python
import functools
import types

import jax
import jax.numpy as jnp
from jax import lax
from jax.experimental import pallas as pl
from jax.experimental.pallas import tpu as pltpu
from jax.sharding import PartitionSpec as P


SEQ = "seq"
HEAD = "head"
DK = 128
DV = 256
CONV = 4
STACK_LEVELS = 2
QKV = 2 * DK + DV
WIDE = 2 * DK + 2 * DV
HALF = DV // 2
PAD = 8

f32 = jnp.float32
bf16 = jnp.bfloat16
norm_eps = 1e-06
gate_unit = 1.0 / 1048576.0
beta_unit = 1.0 / 1024.0


def shape_of(dims, dtype=f32):
    return jax.ShapeDtypeStruct(tuple(dims), dtype)


def call(body, outs, args, scratch=()):
    specs, arrays = [], []
    for arg in args:
        if isinstance(arg, tuple):
            array, level = arg
            rest = (0,) * (array.ndim - 1)
            specs.append(
                pl.BlockSpec((None,) + array.shape[1:], functools.partial(at_level, level, rest))
            )
        elif arg.dtype == jnp.int32:
            array = arg
            specs.append(pl.BlockSpec(memory_space=pltpu.SMEM))
        else:
            array = arg
            specs.append(pl.BlockSpec(memory_space=pltpu.VMEM))
        arrays.append(array)
    return pl.pallas_call(
        body,
        grid=(1,),
        out_shape=tuple(outs),
        in_specs=specs,
        out_specs=tuple(pl.BlockSpec(memory_space=pltpu.VMEM) for _ in outs),
        scratch_shapes=list(scratch),
    )(*arrays)


def at_level(level, rest, _):
    return (level,) + rest


def mm(a, b, ca, cb):
    a_high, b_high = a.astype(bf16), b.astype(bf16)
    a_low = (a - a_high.astype(f32)).astype(bf16)
    b_low = (b - b_high.astype(f32)).astype(bf16)
    return mmb(a_high, b_high, ca, cb) + (mmb(a_high, b_low, ca, cb) + mmb(a_low, b_high, ca, cb))


def mmb(a, b, ca, cb):
    return lax.dot_general(
        a.astype(bf16), b.astype(bf16), (((ca,), (cb,)), ((), ())), preferred_element_type=f32
    )


def sigmoid(u):
    return 1.0 / (1.0 + jnp.exp(-u))


def norm_forward(x, gain):
    return x * lax.rsqrt(jnp.mean(x * x, axis=-1, keepdims=True) + norm_eps) * gain


def norm_backward(x, gain, grad):
    rate = lax.rsqrt(jnp.mean(x * x, axis=-1, keepdims=True) + norm_eps)
    unit = x * rate
    grad_gain = jnp.sum(grad * unit, axis=0, keepdims=True)
    scaled = grad * gain
    grad_x = rate * (scaled - unit * jnp.mean(scaled * unit, axis=-1, keepdims=True))
    return grad_x, grad_gain


def blocks_of(array, parity, size):
    block = array.shape[1] // size
    return jnp.concatenate(
        [array[:, i * block : (i + 1) * block] for i in range(parity, size, 2)], axis=1
    )


def keep_send(array, y, size):
    even, odd = blocks_of(array, 0, size), blocks_of(array, 1, size)
    lead = y == 0
    return jnp.where(lead, even, odd), jnp.where(lead, odd, even)


def put_halves(part, index_ref, part_ref, mine_ref, other_ref):
    rows = part.shape[0] // 2
    bit = index_ref[1]
    part_ref[...] = part
    mine_ref[...] = part_ref[pl.ds(pl.multiple_of(bit * rows, rows), rows), :]
    other_ref[...] = part_ref[pl.ds(pl.multiple_of((1 - bit) * rows, rows), rows), :]


def get_total(index_ref, near_ref, far_ref):
    lead = index_ref[1] == 0
    near, far = near_ref[...], far_ref[...]
    return jnp.concatenate([jnp.where(lead, near, far), jnp.where(lead, far, near)], axis=0)


def in_kernel(
    index_ref, stream_ref, gain_ref, w_ref, keep_ref, send_ref, proj_ref, *, level, size
):
    normed = norm_forward(stream_ref[...].astype(f32), gain_ref[level : level + 1, :])
    keep, send = keep_send(normed, index_ref[0], size)
    keep_ref[...] = keep.astype(bf16)
    send_ref[...] = send.astype(bf16).astype(f32)
    proj_ref[...] = mmb(normed, w_ref[...], 1, 0)


def in_sum_kernel(
    index_ref, mid_ref, near_ref, far_ref, gain_ref, w_ref,
    stream_ref, keep_ref, send_ref, proj_ref, *, level, size
):
    stream_ref[...] = mid_ref[...] + get_total(index_ref, near_ref, far_ref)
    in_kernel(
        index_ref, stream_ref, gain_ref, w_ref, keep_ref, send_ref, proj_ref,
        level=level, size=size,
    )


def conv_of(win_ref, taps, length):
    conv = taps[0:1] * win_ref[pl.ds(PAD, length), :]
    for tap in range(1, CONV):
        conv = conv + taps[tap : tap + 1] * win_ref[pl.ds(PAD - tap, length), :]
    return conv


def decay_of(col, row, length):
    rows = lax.broadcasted_iota(jnp.int32, (length, length), 0)
    cols = lax.broadcasted_iota(jnp.int32, (length, length), 1)
    keep = rows >= cols
    ratio = jnp.where(keep, jnp.exp(jnp.where(keep, col - row, 0.0)), 0.0)
    return rows, cols, ratio


def delta_kernel(
    y_ref, proj_ref, before_ref, taps_ref, col_ref, row_ref, beta_ref,
    ow_ref, uw_ref, solve_ref, mix_ref, send_ref, keep_ref, transfer_ref,
    win_ref, offset_ref,
):
    length = proj_ref.shape[0]
    for head in range(col_ref.shape[0]):
        base = head * WIDE
        win_ref[0:PAD, :] = before_ref[:, base : base + QKV]
        win_ref[pl.ds(PAD, length), :] = proj_ref[:, base : base + QKV]
        conv = conv_of(win_ref, taps_ref[:, head * QKV : (head + 1) * QKV].astype(f32), length)
        active = conv * sigmoid(conv)
        q_act = active[:, :DK]
        k_act = active[:, DK : 2 * DK]
        values = active[:, 2 * DK :]
        q = q_act * lax.rsqrt(jnp.sum(q_act * q_act, axis=-1, keepdims=True) + norm_eps)
        q = q * DK ** (-0.5)
        k = k_act * lax.rsqrt(jnp.sum(k_act * k_act, axis=-1, keepdims=True) + norm_eps)
        col = col_ref[head]
        row = row_ref[head]
        beta = beta_ref[head]
        rows, cols, ratio = decay_of(col, row, length)
        key_key = mm(k, k, 1, 1)
        query_key = mm(q, k, 1, 1)
        lower = jnp.where(rows > cols, beta * ratio * key_key, 0.0)
        solve = jnp.where(rows == cols, 1.0, 0.0)
        block = 1
        while block < length:
            here = (
                (rows // (2 * block) == cols // (2 * block))
                & (rows % (2 * block) >= block)
                & (cols % (2 * block) < block)
            )
            part = jnp.where(here, lower, 0.0)
            if block == 1:
                solve = solve - part
            else:
                solve = solve - mm(solve, mm(part, solve, 1, 0), 1, 0)
            block *= 2
        decay = jnp.exp(col)
        right = jnp.concatenate([beta * values, (beta * decay) * k], axis=1)
        uw = mm(solve, right, 1, 0)
        mix = ratio * query_key
        muw = mm(mix, uw, 1, 0)
        last = row[:, length - 1 :]
        ends = mm(uw, jnp.exp(last - col) * k, 0, 0)
        eye = jnp.where(
            lax.broadcasted_iota(jnp.int32, (DK, DK), 0)
            == lax.broadcasted_iota(jnp.int32, (DK, DK), 1),
            1.0,
            0.0,
        )
        transfer = jnp.exp(last) * eye - ends[DV:]
        offset_ref[...] = ends[:DV]
        ow_ref[head] = jnp.concatenate([muw[:, :DV], decay * q - muw[:, DV:]], axis=1)
        uw_ref[head] = uw
        solve_ref[head] = solve
        mix_ref[head] = mix
        transfer_ref[head] = transfer
        y = y_ref[0]
        send_ref[head, 0:DK, :] = transfer
        send_ref[head, DK : DK + HALF, :] = offset_ref[
            pl.ds(pl.multiple_of((1 - y) * HALF, HALF), HALF), :
        ]
        keep_ref[head] = offset_ref[pl.ds(pl.multiple_of(y * HALF, HALF), HALF), :]


def pair_kernel(
    y_ref, own_ref, keep_ref, other_ref, first_t_ref, second_t_ref, first_o_ref, pair_ref
):
    lead = y_ref[0] == 0
    for head in range(own_ref.shape[0]):
        own, other = own_ref[head], other_ref[head, 0:DK, :]
        keep, far = keep_ref[head], other_ref[head, DK : DK + HALF, :]
        first_t, second_t = jnp.where(lead, own, other), jnp.where(lead, other, own)
        first_o, second_o = jnp.where(lead, keep, far), jnp.where(lead, far, keep)
        first_t_ref[head] = first_t
        second_t_ref[head] = second_t
        first_o_ref[head] = first_o
        both = mm(jnp.concatenate([first_t, first_o], axis=0), second_t, 1, 0)
        pair_ref[head, 0:DK, :] = both[:DK]
        pair_ref[head, DK : DK + HALF, :] = both[DK:] + second_o


def window_kernel(near_ref, pair_ref, out_ref):
    for head in range(pair_ref.shape[0]):
        pair = pair_ref[head]
        out_ref[head] = mm(near_ref[head, DK : DK + HALF, :], pair[:DK], 1, 0) + pair[DK:]


def step_kernel(state_ref, pair_ref, out_ref):
    for head in range(state_ref.shape[0]):
        pair = pair_ref[head]
        out_ref[head] = mm(state_ref[head], pair[:DK], 1, 0) + pair[DK:]


def step_back_kernel(state_ref, pair_ref, offset_ref, out_ref):
    for head in range(state_ref.shape[0]):
        transfer = pair_ref[head, 0:DK, :]
        out_ref[head] = mm(state_ref[head], transfer, 1, 1) + offset_ref[head]


def last_kernel(
    y_ref, state_ref, near_ref, transfer_ref, offset_ref, mine_ref, other_ref, *, window
):
    lead = y_ref[0] == 0
    for head in range(state_ref.shape[0]):
        state = state_ref[head]
        if window:
            near = near_ref[head]
            state = mm(state, near[:DK], 1, 0) + near[DK:]
        moved = mm(state, transfer_ref[head], 1, 0) + offset_ref[head]
        mine_ref[head] = jnp.where(lead, state, moved)
        other_ref[head] = jnp.where(lead, moved, state)


def pair_back_kernel(y_ref, keep_ref, other_ref, first_t_ref, second_ref, pair_ref):
    lead = y_ref[0] == 0
    for head in range(keep_ref.shape[0]):
        keep, far = keep_ref[head], other_ref[head]
        first, second = jnp.where(lead, keep, far), jnp.where(lead, far, keep)
        second_ref[head] = second
        pair_ref[head] = first + mm(second, first_t_ref[head], 1, 1)


def last_back_kernel(y_ref, state_ref, transfer_ref, offset_ref, mine_ref, other_ref):
    lead = y_ref[0] == 0
    for head in range(state_ref.shape[0]):
        state = state_ref[head]
        moved = mm(state, transfer_ref[head], 1, 1) + offset_ref[head]
        mine_ref[head] = jnp.where(lead, moved, state)
        other_ref[head] = jnp.where(lead, state, moved)


def halves(y, mine, other):
    lead = y == 0
    return jnp.concatenate(
        [jnp.where(lead, mine, other), jnp.where(lead, other, mine)], axis=0
    )


def out_kernel(
    y_ref, mine_ref, other_ref, ow_ref, proj_ref, gain_ref, w_ref,
    state_ref, outputs_ref, gated_ref, near_ref, far_ref, part_ref, *, level,
):
    pieces = []
    for head in range(ow_ref.shape[0]):
        state = halves(y_ref[0], mine_ref[head], other_ref[head])
        state_ref[head] = state
        ow = ow_ref[head]
        outputs = ow[:, :DV] + mm(ow[:, DV:], state, 1, 1)
        outputs_ref[:, head * DV : (head + 1) * DV] = outputs
        z = proj_ref[:, head * WIDE + QKV : (head + 1) * WIDE]
        pieces.append((norm_forward(outputs, gain_ref[level : level + 1, :]) * (z * sigmoid(z))).astype(bf16))
    gated = jnp.concatenate(pieces, axis=1)
    gated_ref[...] = gated.astype(f32)
    put_halves(mmb(gated, w_ref[...], 1, 0), y_ref, part_ref, near_ref, far_ref)


def ffn_kernel(
    index_ref, stream_ref, near_ref, far_ref, gain_ref, wg_ref, wu_ref, wd_ref,
    mid_ref, keep_ref, send_ref, gate_ref, up_ref, mine_ref, other_ref, part_ref,
    *, level, size,
):
    mid = stream_ref[...].astype(f32) + get_total(index_ref, near_ref, far_ref)
    mid_ref[...] = mid
    normed = norm_forward(mid, gain_ref[level : level + 1, :])
    keep, send = keep_send(normed, index_ref[0], size)
    keep_ref[...] = keep.astype(bf16)
    half = mid.shape[1] // 2
    send_ref[:, :half] = send.astype(bf16).astype(f32)
    normed = normed.astype(bf16)
    gate = mmb(normed, wg_ref[...], 1, 0)
    up = mmb(normed, wu_ref[...], 1, 0)
    gate_ref[...] = gate
    up_ref[...] = up
    hidden = (gate * sigmoid(gate) * up).astype(bf16)
    send_ref[:, half:] = hidden.astype(f32)
    put_halves(mmb(hidden, wd_ref[...], 1, 0), index_ref, part_ref, mine_ref, other_ref)


def sum_kernel(index_ref, mid_ref, near_ref, far_ref, out_ref):
    out_ref[...] = (mid_ref[...] + get_total(index_ref, near_ref, far_ref)).astype(bf16)


def ffn_back_kernel(
    index_ref, grad_ref, gate_ref, up_ref, wg_ref, wu_ref, wd_ref,
    keep_ref, send_ref, mine_ref, other_ref, part_ref, *, size,
):
    back = grad_ref[...].astype(bf16)
    keep, send = keep_send(back.astype(f32), index_ref[0], size)
    keep_ref[...] = keep.astype(bf16)
    hidden = mmb(back, wd_ref[...], 1, 1)
    gate, up = gate_ref[...], up_ref[...]
    rate = sigmoid(gate)
    gu = (hidden * (gate * rate)).astype(bf16)
    gg = (hidden * up * (rate * (1.0 + gate * (1.0 - rate)))).astype(bf16)
    width = gate.shape[1]
    send_ref[:, : 2 * width] = jnp.concatenate([gg.astype(f32), gu.astype(f32)], axis=1)
    send_ref[:, 2 * width :] = send
    part = mmb(gg, wg_ref[...], 1, 1) + mmb(gu, wu_ref[...], 1, 1)
    put_halves(part, index_ref, part_ref, mine_ref, other_ref)


def out_back_kernel(
    y_ref, grad_ref, near_ref, far_ref, mid_ref, gain_ref, w_ref, outputs_ref, proj_ref,
    out_gain_ref, ow_ref,
    next_ref, back_keep_ref, back_send_ref, do_ref, dz_ref, dgain_ref, dout_gain_ref,
    send_ref, keep_ref,
    local_ref, *, level, size,
):
    grad_mid, grad_gain = norm_backward(
        mid_ref[...], gain_ref[level : level + 1, :], get_total(y_ref, near_ref, far_ref)
    )
    dgain_ref[...] = grad_gain
    grad = grad_ref[...].astype(f32) + grad_mid
    next_ref[...] = grad
    back = grad.astype(bf16)
    back_keep, back_send = keep_send(back.astype(f32), y_ref[0], size)
    back_keep_ref[...] = back_keep.astype(bf16)
    back_send_ref[...] = back_send
    gated = mmb(back, w_ref[...], 1, 1)
    gain = out_gain_ref[level : level + 1, :]
    total_gain = jnp.zeros_like(gain)
    y = y_ref[0]
    for head in range(ow_ref.shape[0]):
        span = slice(head * DV, (head + 1) * DV)
        outputs = outputs_ref[:, span]
        z = proj_ref[:, head * WIDE + QKV : (head + 1) * WIDE]
        rate = sigmoid(z)
        grad_h = gated[:, span]
        grad_n = grad_h * (z * rate)
        dz_ref[:, span] = (
            grad_h * norm_forward(outputs, gain) * (rate * (1.0 + z * (1.0 - rate)))
        )
        grad_o, gain_part = norm_backward(outputs, gain, grad_n)
        total_gain = total_gain + gain_part
        do_ref[:, span] = grad_o
        local_ref[...] = mm(grad_o, ow_ref[head][:, DV:], 0, 0)
        send_ref[head] = local_ref[pl.ds(pl.multiple_of((1 - y) * HALF, HALF), HALF), :]
        keep_ref[head] = local_ref[pl.ds(pl.multiple_of(y * HALF, HALF), HALF), :]
    dout_gain_ref[...] = total_gain


def delta_back_kernel(
    y_ref, mine_ref, other_ref, state_ref, uw_ref, solve_ref, mix_ref, do_ref,
    proj_ref, before_ref, taps_ref, col_ref, row_ref, beta_ref,
    dconv_ref, dtaps_ref, edge_ref,
    win_ref,
):
    length = proj_ref.shape[0]
    for head in range(col_ref.shape[0]):
        base = head * WIDE
        win_ref[0:PAD, :] = before_ref[:, base : base + QKV]
        win_ref[pl.ds(PAD, length), :] = proj_ref[:, base : base + QKV]
        taps = taps_ref[:, head * QKV : (head + 1) * QKV].astype(f32)
        conv = conv_of(win_ref, taps, length)
        rate = sigmoid(conv)
        active = conv * rate
        q_act = active[:, :DK]
        k_act = active[:, DK : 2 * DK]
        q_rate = lax.rsqrt(jnp.sum(q_act * q_act, axis=-1, keepdims=True) + norm_eps)
        k_rate = lax.rsqrt(jnp.sum(k_act * k_act, axis=-1, keepdims=True) + norm_eps)
        q_unit = q_act * q_rate
        k = k_act * k_rate
        q = q_unit * DK ** (-0.5)
        col = col_ref[head]
        row = row_ref[head]
        beta = beta_ref[head]
        rows, cols, ratio = decay_of(col, row, length)
        decay = jnp.exp(col)
        to_end = jnp.exp(row[:, length - 1 :] - col)
        state = state_ref[head]
        grad_end = halves(y_ref[0], mine_ref[head], other_ref[head])
        uw = uw_ref[head]
        grad_o = do_ref[:, head * DV : (head + 1) * DV]
        values_new = uw[:, :DV] - mmb(uw[:, DV:], state, 1, 1)
        grad_new = mmb(mix_ref[head], grad_o, 0, 0) + mmb(to_end * k, grad_end, 1, 1)
        grad_right = mmb(solve_ref[head], grad_new, 0, 0)
        grad_mix = jnp.where(rows >= cols, ratio * mmb(grad_o, values_new, 1, 1), 0.0)
        grad_low = jnp.where(
            rows > cols, -(beta * ratio) * mmb(grad_right, values_new, 1, 1), 0.0
        )
        grad_q = decay * mmb(grad_o, state, 1, 0) + mmb(grad_mix, k, 1, 0)
        grad_k = to_end * mmb(values_new, grad_end, 1, 0)
        grad_k = grad_k - (beta * decay) * mmb(grad_right, state, 1, 0)
        grad_k = grad_k + mmb(grad_low, k, 1, 0) + mmb(grad_low, k, 0, 0)
        grad_k = grad_k + mmb(grad_mix, q, 0, 0)
        grad_v = beta * grad_right
        grad_qa = (DK ** (-0.5)) * q_rate * (
            grad_q - q_unit * jnp.sum(grad_q * q_unit, axis=-1, keepdims=True)
        )
        grad_ka = k_rate * (grad_k - k * jnp.sum(grad_k * k, axis=-1, keepdims=True))
        grad_conv = jnp.concatenate([grad_qa, grad_ka, grad_v], axis=1) * (
            rate * (1.0 + conv * (1.0 - rate))
        )
        span = slice(head * QKV, (head + 1) * QKV)
        dconv_ref[:, span] = grad_conv
        edge_ref[:, span] = grad_conv[0:PAD]
        for tap in range(CONV):
            dtaps_ref[tap : tap + 1, span] = jnp.sum(
                grad_conv * win_ref[pl.ds(PAD - tap, length), :], axis=0, keepdims=True
            )


def in_back_kernel(
    index_ref, dconv_ref, after_ref, taps_ref, dz_ref, w_ref,
    gp_ref, mine_ref, other_ref, ext_ref, part_ref,
):
    length = dconv_ref.shape[0]
    ext_ref[pl.ds(0, length), :] = dconv_ref[...]
    ext_ref[pl.ds(length, PAD), :] = after_ref[...]
    taps = taps_ref[...].astype(f32)
    total = taps[0:1] * ext_ref[pl.ds(0, length), :]
    for tap in range(1, CONV):
        total = total + taps[tap : tap + 1] * ext_ref[pl.ds(tap, length), :]
    pieces = []
    for head in range(total.shape[1] // QKV):
        pieces.append(total[:, head * QKV : (head + 1) * QKV])
        pieces.append(dz_ref[:, head * DV : (head + 1) * DV])
    grad_proj = jnp.concatenate(pieces, axis=1).astype(bf16)
    gp_ref[...] = grad_proj.astype(f32)
    put_halves(mmb(grad_proj, w_ref[...], 1, 1), index_ref, part_ref, mine_ref, other_ref)


def norm_back_kernel(
    index_ref, grad_ref, near_ref, far_ref, stream_ref, gain_ref, out_ref, dgain_ref, *, level
):
    grad_x, grad_gain = norm_backward(
        stream_ref[...].astype(f32),
        gain_ref[level : level + 1, :],
        get_total(index_ref, near_ref, far_ref),
    )
    out_ref[...] = grad_ref[...] + grad_x
    dgain_ref[...] = grad_gain


def weight_block_kernel(
    n2_ref, own_ref, own_far_ref, ffn_ref, ffn_far_ref, back_ref, mid_ref, mid_far_ref,
    gated_ref, gated_far_ref, out_ref,
):
    half = back_ref.shape[1]
    width = own_ref.shape[1] - half
    both = 2 * width
    out_ref[:, :both] = mmb(n2_ref[...], ffn_ref[:, :both], 0, 0) + mmb(
        own_far_ref[:, :half], ffn_far_ref[:, :both], 0, 0
    )
    out_ref[:, both : both + width] = mmb(back_ref[...], own_ref[:, half:], 0, 0) + mmb(
        ffn_far_ref[:, both:], own_far_ref[:, half:], 0, 0
    )
    out_ref[:, both + width :] = mmb(mid_ref[...], gated_ref[...], 0, 0) + mmb(
        mid_far_ref[...], gated_far_ref[...], 0, 0
    )


def weight_in_kernel(a_ref, b_ref, a_far_ref, b_far_ref, out_ref):
    out_ref[...] = mmb(a_ref[...], b_ref[...], 0, 0) + mmb(a_far_ref[...], b_far_ref[...], 0, 0)


def shift(array, axis, by):
    length = lax.axis_size(axis)
    pairs = [(i, i + by) for i in range(length) if 0 <= i + by < length]
    return lax.ppermute(array, axis, pairs)


def swap(array, axis, bit):
    length = lax.axis_size(axis)
    return lax.ppermute(array, axis, [(i, i ^ bit) for i in range(length)])


def head_total(mine, other):
    total = mine + swap(other, HEAD, 1)
    step = 2
    while step < lax.axis_size(HEAD):
        total = total + swap(total, HEAD, step)
        step *= 2
    return total, swap(total, HEAD, 1)


def far_swap(array):
    return swap(array, SEQ, 1)


def after(array, mark):
    return lax.optimization_barrier((array, mark))[0]


def full_sum(array, axis):
    step = 1
    while step < lax.axis_size(axis):
        array = array + swap(array, axis, step)
        step *= 2
    return array


def outer_scatter(array):
    size = lax.axis_size(SEQ)
    groups = [[2 * o + p for o in range(size // 2)] for p in range(2)]
    return lax.psum_scatter(array, SEQ, scatter_dimension=0, tiled=True, axis_index_groups=groups)


def prefix(local, transfer, y):
    send, keep = local
    heads = keep.shape[0]
    square = shape_of((heads, DK, DK))
    half = shape_of((heads, HALF, DK))
    outer = lax.axis_size(SEQ) // 2
    far = swap(send, SEQ, 1)
    first_t, second_t, first_o, pair = call(
        pair_kernel,
        [square, square, half, shape_of((heads, DK + HALF, DK))],
        [y, transfer, keep, far],
    )
    if outer == 4:
        near = shift(pair, SEQ, 2)
        (moved,) = call(window_kernel, [half], [near, pair])
        state = shift(moved, SEQ, 4)
    else:
        near = pair
        state = shift(pair[:, DK:], SEQ, 2)
        for _ in range(outer - 2):
            (moved,) = call(step_kernel, [half], [state, pair])
            state = shift(moved, SEQ, 2)
    mine, other = call(
        functools.partial(last_kernel, window=outer == 4),
        [half, half],
        [y, state, near, first_t, first_o],
    )
    return mine, swap(other, SEQ, 1), first_t, second_t, pair, near


def suffix(send, keep, kept, y):
    heads = keep.shape[0]
    half = shape_of((heads, HALF, DK))
    outer = lax.axis_size(SEQ) // 2
    far = swap(send, SEQ, 1)
    second_o, pair_o = call(pair_back_kernel, [half, half], [y, keep, far, kept.first_t])
    state = shift(pair_o, SEQ, -2)
    mark = pair_o
    for _ in range(outer - 2):
        (moved,) = call(step_back_kernel, [half], [state, kept.pair, pair_o])
        state = shift(moved, SEQ, -2)
    mine, other = call(last_back_kernel, [half, half], [y, state, kept.second_t, second_o])
    return mine, swap(other, SEQ, 1), mark


def layer_forward(start, shared, level, y):
    col, row, beta, gain_one, w_in, taps, out_gain, w_out, gain_two, w_gate, w_up, w_down = shared
    length, width = start[0].shape
    heads = col.shape[1]
    proj_width = w_in.shape[2]
    hidden_width = w_gate.shape[2]
    value_width = heads * DV
    size = lax.axis_size(SEQ)
    half_width = width // 2
    rows = shape_of((length // 2, width))
    whole = pltpu.VMEM((length, width), f32)
    kept_half = [shape_of((length, half_width), bf16), shape_of((length, half_width))]
    if len(start) == 1:
        stream = start[0]
        normed, normed_send, proj = call(
            functools.partial(in_kernel, level=level, size=size),
            kept_half + [shape_of((length, proj_width))],
            [y, stream, gain_one, (w_in, level)],
        )
    else:
        stream, normed, normed_send, proj = call(
            functools.partial(in_sum_kernel, level=level, size=size),
            [shape_of((length, width))] + kept_half + [shape_of((length, proj_width))],
            [y, *start, gain_one, (w_in, level)],
        )
    before = shift(proj[length - PAD :], SEQ, 1)
    square = shape_of((heads, DK, DK))
    wide = shape_of((heads, length, DV + DK))
    inner = shape_of((heads, length, length))
    half = shape_of((heads, HALF, DK))
    ow, uw, solve, mix, send, keep, transfer = call(
        delta_kernel,
        [wide, wide, inner, inner, shape_of((heads, DK + HALF, DK)), half, square],
        [y, proj, before, (taps, level), (col, level), (row, level), (beta, level)],
        [pltpu.VMEM((length + PAD, QKV), f32), pltpu.VMEM((DV, DK), f32)],
    )
    mine, other, first_t, second_t, pair, _ = prefix((send, keep), transfer, y)
    incoming, outputs, gated, near, far = call(
        functools.partial(out_kernel, level=level),
        [
            shape_of((heads, DV, DK)),
            shape_of((length, value_width)),
            shape_of((length, value_width)),
            rows,
            rows,
        ],
        [y, mine, other, ow, proj, out_gain, (w_out, level)],
        [whole],
    )
    total = head_total(near, far)
    mid, normed_two, ffn_send, gate, up, near, far = call(
        functools.partial(ffn_kernel, level=level, size=size),
        [
            shape_of((length, width)),
            shape_of((length, half_width), bf16),
            shape_of((length, half_width + hidden_width)),
            shape_of((length, hidden_width)),
            shape_of((length, hidden_width)),
            rows,
            rows,
        ],
        [y, stream, *total, gain_two, (w_gate, level), (w_up, level), (w_down, level)],
        [whole],
    )
    total = head_total(near, far)
    stored = types.SimpleNamespace(
        stream=stream, normed=normed, proj=proj, before=before, ow=ow, uw=uw, solve=solve,
        mix=mix, first_t=first_t, second_t=second_t, pair=pair, incoming=incoming,
        outputs=outputs, gated=gated, mid=mid, normed_two=normed_two, gate=gate, up=up,
        ffn_send=ffn_send, normed_far=far_swap(after(normed_send, gated)),
        gated_far=far_swap(gated), ffn_far=far_swap(ffn_send),
    )
    return (mid, *total), stored


def layer_backward(grad, shared, level, kept, y, pending):
    col, row, beta, gain_one, w_in, taps, out_gain, w_out, gain_two, w_gate, w_up, w_down = shared
    length, width = grad.shape
    heads = col.shape[1]
    proj_width = w_in.shape[2]
    hidden_width = w_gate.shape[2]
    value_width = heads * DV
    qkv_width = heads * QKV
    size = lax.axis_size(SEQ)
    half_width = width // 2
    rows = shape_of((length // 2, width))
    whole = pltpu.VMEM((length, width), f32)
    back, back_send, near, far = call(
        functools.partial(ffn_back_kernel, size=size),
        [
            shape_of((length, half_width), bf16),
            shape_of((length, 2 * hidden_width + half_width)),
            rows,
            rows,
        ],
        [y, grad, kept.gate, kept.up, (w_gate, level), (w_up, level), (w_down, level)],
        [whole],
    )
    back_far = far_swap(back_send)
    total = head_total(near, far)
    if pending is not None:
        pending = pending(near)
    half = shape_of((heads, HALF, DK))
    grad, mid_back, mid_send, grad_o, grad_z, dgain_two, dout_gain, send, keep = call(
        functools.partial(out_back_kernel, level=level, size=size),
        [
            shape_of((length, width)),
            shape_of((length, half_width), bf16),
            shape_of((length, half_width)),
            shape_of((length, value_width)),
            shape_of((length, value_width)),
            shape_of((1, width)),
            shape_of((1, DV)),
            half,
            half,
        ],
        [
            y, grad, *total, kept.mid, gain_two, (w_out, level), kept.outputs,
            kept.proj, out_gain, kept.ow,
        ],
        [pltpu.VMEM((DV, DK), f32)],
    )
    mid_far = far_swap(mid_send)
    mine, other, mark = suffix(send, keep, kept, y)
    (block_weights,) = call(
        weight_block_kernel,
        [shape_of((half_width, 3 * hidden_width + value_width))],
        [
            kept.normed_two, kept.ffn_send, kept.ffn_far, back_send,
            after(back_far, mark), back, mid_back, mid_far, kept.gated, kept.gated_far,
        ],
    )
    block_weights = outer_scatter(block_weights)
    dconv, dtaps, edge = call(
        delta_back_kernel,
        [
            shape_of((length, qkv_width)),
            shape_of((CONV, qkv_width)),
            shape_of((PAD, qkv_width)),
        ],
        [
            y, mine, other, kept.incoming, kept.uw, kept.solve, kept.mix, grad_o,
            kept.proj, kept.before, (taps, level), (col, level), (row, level),
            (beta, level),
        ],
        [pltpu.VMEM((length + PAD, QKV), f32)],
    )
    grad_proj, near, far = call(
        in_back_kernel,
        [shape_of((length, proj_width)), rows, rows],
        [y, dconv, shift(edge, SEQ, -1), (taps, level), grad_z, (w_in, level)],
        [pltpu.VMEM((length + PAD, qkv_width), f32), whole],
    )
    proj_far = far_swap(grad_proj)

    def finish(mark):
        held = proj_far if mark is None else after(proj_far, mark)
        (in_weights,) = call(
            weight_in_kernel,
            [shape_of((half_width, proj_width))],
            [kept.normed, grad_proj, kept.normed_far, held],
        )
        return outer_scatter(in_weights)

    total = head_total(near, far)
    grad, dgain_one = call(
        functools.partial(norm_back_kernel, level=level),
        [shape_of((length, width)), shape_of((1, width))],
        [y, grad, *total, kept.stream, gain_one],
    )
    return grad, (block_weights, dtaps, dgain_one, dout_gain, dgain_two), finish, pending


def body(
    tokens,
    cotangent,
    gate_code,
    beta_code,
    norm1_gain,
    weight_in,
    conv_weight,
    out_gain,
    weight_out,
    norm2_gain,
    weight_gate,
    weight_up,
    weight_down,
):
    y = jnp.stack([lax.axis_index(SEQ) % 2, lax.axis_index(HEAD) % 2]).astype(jnp.int32)
    logdecay = -gate_code.astype(f32) * gate_unit
    beta_rate = jnp.transpose(beta_code.astype(f32) * beta_unit, (0, 2, 1))
    cumulated = jnp.transpose(jnp.cumsum(logdecay, axis=1), (0, 2, 1))
    shared = (
        cumulated[:, :, :, None],
        cumulated[:, :, None, :],
        beta_rate[:, :, :, None],
        norm1_gain,
        weight_in,
        conv_weight,
        out_gain,
        weight_out,
        norm2_gain,
        weight_gate,
        weight_up,
        weight_down,
    )
    start = (tokens,)
    kept = []
    for level in range(STACK_LEVELS):
        start, stored = layer_forward(start, shared, level, y)
        kept.append(stored)
    grad = cotangent
    parts = [None] * STACK_LEVELS
    in_weights = [None] * STACK_LEVELS
    finish = None
    for level in reversed(range(STACK_LEVELS)):
        grad, parts[level], finish, done = layer_backward(
            grad, shared, level, kept[level], y, finish
        )
        if done is not None:
            in_weights[level + 1] = done
    in_weights[0] = finish(None)
    (activations,) = call(sum_kernel, [shape_of(tokens.shape, bf16)], [y, *start])
    hidden_width = weight_gate.shape[2]
    block = [part[0] for part in parts]

    def join(pick):
        return jnp.stack([pick(piece) for piece in block])

    grad_gate = join(lambda piece: piece[:, :hidden_width])
    grad_up = join(lambda piece: piece[:, hidden_width : 2 * hidden_width])
    grad_down = join(lambda piece: piece[:, 2 * hidden_width : 3 * hidden_width].T)
    grad_out = join(lambda piece: piece[:, 3 * hidden_width :].T)
    grad_in = jnp.stack(in_weights)
    qkv_width = conv_weight.shape[2]
    width = tokens.shape[1]
    out_gain_part = full_sum(jnp.concatenate([part[3] for part in parts], axis=0), HEAD)
    small = jnp.concatenate(
        [part[1].reshape(1, -1) for part in parts]
        + [part[2] for part in parts]
        + [part[4] for part in parts]
        + [out_gain_part.reshape(1, -1)],
        axis=1,
    )
    small = full_sum(small, SEQ)[0]
    sizes = [STACK_LEVELS * CONV * qkv_width, STACK_LEVELS * width, STACK_LEVELS * width]
    conv_grad = small[: sizes[0]].reshape(STACK_LEVELS, CONV, qkv_width)
    gain_one_grad = small[sizes[0] : sizes[0] + sizes[1]].reshape(STACK_LEVELS, width)
    gain_two_grad = small[sizes[0] + sizes[1] : sum(sizes)].reshape(STACK_LEVELS, width)
    out_gain_grad = small[sum(sizes) :].reshape(STACK_LEVELS, DV)
    return (
        activations,
        grad,
        gain_one_grad,
        grad_in,
        conv_grad,
        out_gain_grad,
        grad_out,
        gain_two_grad,
        grad_gate,
        grad_up,
        grad_down,
    )


def solution(mesh):
    in_specs = (
        P(SEQ, None),
        P(SEQ, None),
        P(None, SEQ, HEAD),
        P(None, SEQ, HEAD),
        P(),
        P(None, None, HEAD),
        P(None, None, HEAD),
        P(),
        P(None, HEAD, None),
        P(),
        P(None, None, HEAD),
        P(None, None, HEAD),
        P(None, HEAD, None),
    )
    out_specs = (
        P(SEQ, None),
        P(SEQ, None),
        P(),
        P(None, SEQ, HEAD),
        P(None, None, HEAD),
        P(),
        P(None, HEAD, SEQ),
        P(),
        P(None, SEQ, HEAD),
        P(None, SEQ, HEAD),
        P(None, HEAD, SEQ),
    )

    return jax.shard_map(body, mesh=mesh, in_specs=in_specs, out_specs=out_specs, check_vma=False)
```
